256 devices in a mesh: row: 16 (over x, z_hi, core), loop: 16 (over y, z_lo).
Axes of the slice: x: 4, y: 4, z: 8 (z_hi: 2, z_lo: 4; z = z_hi * 4 + z_lo), core: 2. Of those that a mesh axis runs over, the one named last changes fastest.
Arguments:
- amplitudes: float32 [32768, 12288], P('row', 'loop'), may hold values from -6 to 6
- integrals: float32 [32768, 2048], P('row', 'loop'), may hold values from -0.046875 to 0.046875
- screen_mask: int32 [256, 16], P('row'), may hold values 0 or 1
- base_residual: float32 [2048, 12288], P('row', 'loop'), may hold values from -6 to 6
- vir_energy: float32 [2048], P('row'), may hold values from 0.5 to 4
- occ_energy: float32 [12288], P('loop'), may hold values from 0.5 to 2
Outputs:
- residual: float32 [2048, 12288], P('row', 'loop')
- update: float32 [2048, 12288], P('row', 'loop')
The draws below stay inside these ranges and needn't reach their ends.
All inputs are finite; a program needn't handle non-finite values. No bound on the sum of `screen_mask` on one device may be relied on, other than what follows from the above.
Results may differ from the reference program's by a relative error of at most 0.000068.
Values sent between devices are 32-bit elements; how exact they have to be, the bound alone decides.
A program may use at most 128 MiB of HBM per device.

```python
import math
import jax
import jax.numpy as jnp
from jax import lax

TILE = 128
AB = 2048
CD = 32768
IJ = 12288


def with_ends(result, rng, low, largest):
    shape = result.shape
    index_at = [jax.random.randint(jax.random.fold_in(rng, axis), (), 0, shape[axis]) for axis in range(len(shape))]
    result = result.at[tuple(index_at)].set(low)
    longest = shape.index(max(shape))
    index_at[longest] = (index_at[longest] + 1) % shape[longest]
    return result.at[tuple(index_at)].set(largest)


def level_of(own_key, dims, cuts, least, high):
    gain = 1.0
    for position, blocks in cuts:
        draws = jax.random.uniform(jax.random.fold_in(jax.random.fold_in(own_key, 6), position), (blocks,), jnp.float32, least / len(cuts), high / len(cuts))
        gain = gain * jnp.repeat(jnp.exp(draws), dims[position] // blocks).reshape((-1,) + (1,) * (len(dims) - 1 - position))
    return gain


def bell_draw(own_key, dims, deviation, reach, pieces=(), dtype=jnp.bfloat16):
    gain = level_of(own_key, dims, pieces, -0.22, 0.18) if pieces else 1.0
    result = jax.random.normal(own_key, dims, jnp.float32) * deviation * gain
    return jnp.minimum(jnp.maximum(result, -reach), reach).astype(dtype)


def setup_inputs(seed: int = 0) -> dict:
    arg_keys = jax.random.split(jax.random.key(seed), 7)
    amplitudes = bell_draw(arg_keys[0], (CD, IJ), 1.0, 6.0, ((0, 16), (1, 16)), jnp.float32)
    integrals = bell_draw(arg_keys[1], (CD, AB), (CD // 2) ** -0.5, 0.046875, ((0, 16), (1, 16)), jnp.float32)
    screen_mask = with_ends((jax.random.randint(arg_keys[2], (CD // TILE, AB // TILE), 0, 2) < 1).astype(jnp.int32), jax.random.fold_in(arg_keys[2], 1), 0, 1)
    base_residual = bell_draw(arg_keys[3], (AB, IJ), 1.0, 6.0, ((0, 16), (1, 16)), jnp.float32)
    vir_energy = jnp.clip(jnp.exp(math.log(4.0) - 2.0794415 * jax.random.uniform(arg_keys[4], (AB,), jnp.float32) ** level_of(arg_keys[4], (AB,), ((0, 16),), -0.2, 0.2)), 0.5, 4.0)
    occ_energy = jnp.clip(jnp.exp(math.log(2.0) - 1.3862944 * jax.random.uniform(arg_keys[5], (IJ,), jnp.float32) ** level_of(arg_keys[5], (IJ,), ((0, 16),), -0.2, 0.2)), 0.5, 2.0)
    return {"amplitudes": amplitudes, "integrals": integrals, "screen_mask": screen_mask, "base_residual": base_residual, "vir_energy": vir_energy, "occ_energy": occ_energy}


def expand_mask(screen_mask, tile):
    rows_t, cols_t = screen_mask.shape
    values = screen_mask.astype(jnp.float32)
    return jnp.broadcast_to(values[:, None, :, None], (rows_t, tile, cols_t, tile)).reshape(rows_t * tile, cols_t * tile)


def reference(amplitudes, integrals, screen_mask, base_residual, vir_energy, occ_energy):
    screened = integrals * expand_mask(screen_mask, TILE)
    ladder = lax.dot_general(screened, amplitudes, (((0,), (0,)), ((), ())), precision=lax.Precision.HIGHEST, preferred_element_type=jnp.float32)
    residual = base_residual + ladder
    update = residual / (vir_energy[:, None] + occ_energy[None, :])
    return residual, update
```

```python
import jax
import jax.numpy as jnp
from jax import lax
from jax.experimental import pallas as pl
from jax.experimental.pallas import tpu as pltpu
from jax.sharding import PartitionSpec as P

TILE = 128
NL = 16
CR = 2048
HALF = CR // 2
IC = 768
BF = jnp.bfloat16
F32 = jnp.float32
MESH = pl.DeviceIdType.MESH


def kernel(
    amp_hbm,
    int_hbm,
    mask,
    out,
    blk,
    t32,
    tth,
    ttl,
    rhs,
    pbuf,
    crecv,
    xrecv,
    zrecv,
    load_sem,
    g_recv,
    y_send,
    yf_send,
    z_send,
    zf_send,
    c_send,
    c_recv,
    x_send,
    x_recv,
    h_send,
    h_recv,
):
    row = lax.axis_index("row")
    loop = lax.axis_index("loop")
    x, zh, core = row // 4, (row // 2) % 2, row % 2
    y, z = loop // 4, loop % 4
    zq = z // 2
    inner = ((z + 1) // 2) % 2 == 1
    ys = [y, (y + 1) % 4, (y + 3) % 4, (y + 2) % 4]
    zs = [z, z + 1 - 2 * (z % 2), 2 - zq, 3 - 3 * zq]

    def slot(d, k):
        return ys[d] * 4 + zs[k]

    up = (row, ys[1] * 4 + z)
    down = (row, ys[2] * 4 + z)
    znear = (row, y * 4 + zs[1])
    zfar = (row, y * 4 + 3 - z)
    mate = (row + 1 - 2 * core, loop)
    hpeer = (row + 2 - 4 * zh, loop)

    barrier = pltpu.get_barrier_semaphore()
    peers = [up, down, znear, mate, hpeer]
    peers += [(((x + j) % 4) * 4 + zh * 2 + core, loop) for j in (1, 2, 3)]
    for peer in peers:
        pl.semaphore_signal(barrier, inc=1, device_id=peer, device_id_type=MESH)

    @pl.when(inner)
    def _():
        pl.semaphore_signal(barrier, inc=1, device_id=zfar, device_id_type=MESH)

    load_t = pltpu.make_async_copy(amp_hbm, t32, load_sem.at[0])
    load_t.start()
    load_b = pltpu.make_async_copy(int_hbm, blk.at[loop], load_sem.at[1])
    load_b.start()
    pl.semaphore_wait(barrier, len(peers) + ((z + 1) // 2) % 2)

    def remote(src, dst, send, recv, to):
        return pltpu.make_async_remote_copy(
            src_ref=src,
            dst_ref=dst,
            send_sem=send,
            recv_sem=recv,
            device_id=to,
            device_id_type=MESH,
        )

    def g_copy(s, h, send, to, own=False):
        src = int_hbm.at[h] if own else blk.at[s, h]
        return remote(src, blk.at[s, h], send, g_recv.at[s, h], to)

    def arrived(d, k, h):
        s = slot(d, k)
        g_copy(s, h, y_send.at[0, 0, 0], up).wait_recv()

    def y_copies(k):
        s = slot(0, k)
        own = k == 0
        return [
            g_copy(s, 0, y_send.at[0, k, 0], up, own),
            g_copy(s, 1, y_send.at[1, k, 1], down, own),
            g_copy(s, 1, y_send.at[0, k, 1], up, own),
            g_copy(s, 0, y_send.at[1, k, 0], down, own),
        ]

    def zf_copies(k):
        s = slot(0, k)
        to = znear if k > 1 else zfar
        return [g_copy(s, h, zf_send.at[k - 1, h], to) for h in (0, 1)]

    def z_copies(far):
        to = zfar if far else znear
        return [g_copy(loop, h, z_send.at[far, h], to, True) for h in (0, 1)]

    def f_copies(k):
        return [
            g_copy(slot(2, k), 0, yf_send.at[0, k], up),
            g_copy(slot(1, k), 1, yf_send.at[1, k], down),
        ]

    for c in z_copies(0):
        c.start()

    @pl.when(inner)
    def _():
        for c in z_copies(1):
            c.start()

    for c in y_copies(0):
        c.start()

    load_t.wait()

    def prep(j, carry):
        at = pl.multiple_of(j * 128, 128)
        t = t32[pl.ds(at, 128), :].T
        hi = t.astype(BF)
        tth[:, pl.ds(at, 128)] = hi
        ttl[:, pl.ds(at, 128)] = (t - hi.astype(F32)).astype(BF)
        return carry

    lax.fori_loop(0, CR // 128, prep, 0)

    def compute(d, k):
        s = slot(d, k)

        def split(j, carry):
            h, at = j // 8, pl.multiple_of((j % 8) * 128, 128)
            m = blk[s, h, pl.ds(at, 128), :] * mask[j, s].astype(F32)
            hi = m.astype(BF)
            lo = (m - hi.astype(F32)).astype(BF)
            to = pl.multiple_of(j * 128, 128)
            rhs[pl.ds(to, 128), 0:128] = hi
            rhs[pl.ds(to, 128), 128:256] = lo
            return carry

        lax.fori_loop(0, 16, split, 0)

        def rows(j, carry):
            at = pl.multiple_of(j * 256, 256)
            a = jnp.dot(tth[pl.ds(at, 256), :], rhs[...], preferred_element_type=F32)
            b = jnp.dot(ttl[pl.ds(at, 256), :], rhs[:, 0:128], preferred_element_type=F32)
            pbuf[s, pl.ds(at, 256), :] = a[:, 0:128] + (a[:, 128:256] + b)
            return carry

        lax.fori_loop(0, IC // 256, rows, 0)

        @pl.when((zs[k] + core) % 2 == 1)
        def _():
            c_copy(d, k // 2, s).start()

    def c_copy(d, p, s):
        n = d * 2 + p
        return remote(pbuf.at[s], crecv.at[n], c_send.at[n], c_recv.at[n], mate)

    def keep_slot(yv, p):
        return yv * 4 + 2 * ((zq + p) % 2) + core

    def x_copy(d, p):
        yv = ys[d]
        s = keep_slot(yv, p)
        place = (x + 4 - yv) % 4 - 1
        to = (yv * 4 + zh * 2 + core, loop)
        return remote(
            pbuf.at[s], xrecv.at[place, p], x_send.at[d, p], x_recv.at[place, p], to
        )

    def reduce_pair(d, p):
        n = d * 2 + p
        s = keep_slot(ys[d], p)
        c_copy(d, p, s).wait_recv()
        pbuf[s] = pbuf[s] + crecv[n]

        @pl.when(x != ys[d])
        def _():
            x_copy(d, p).start()

    def y_out(k):
        for c in y_copies(k):
            c.start()

    def z_forward(k):
        for h in (0, 1):
            arrived(0, k, h)

        @pl.when(inner)
        def _():
            for c in zf_copies(k):
                c.start()

    def y_forward(k):
        arrived(2, k, 0)
        up_c, down_c = f_copies(k)
        up_c.start()
        arrived(1, k, 1)
        down_c.start()

    def rest(k):
        arrived(1, k, 0)
        arrived(2, k, 1)

    def last(k):
        arrived(3, k, 0)
        arrived(3, k, 1)

    load_b.wait()
    compute(0, 0)
    z_forward(1)
    y_out(1)
    y_forward(0)
    rest(0)
    compute(0, 1)
    compute(1, 0)
    compute(2, 0)
    reduce_pair(0, 0)
    z_forward(2)
    y_out(2)
    y_forward(1)
    rest(1)
    compute(0, 2)
    compute(1, 1)
    compute(2, 1)
    reduce_pair(1, 0)
    last(0)
    compute(3, 0)
    reduce_pair(2, 0)
    z_forward(3)
    y_out(3)
    compute(0, 3)
    y_forward(2)
    rest(2)
    compute(1, 2)
    reduce_pair(0, 1)
    compute(2, 2)
    last(1)
    compute(3, 1)
    y_forward(3)
    reduce_pair(3, 0)
    rest(3)
    compute(1, 3)
    compute(2, 3)
    reduce_pair(1, 1)
    last(2)
    compute(3, 2)
    reduce_pair(2, 1)
    last(3)
    compute(3, 3)
    reduce_pair(3, 1)

    def x_total(p):
        s = keep_slot(x, p)
        for j in range(3):
            remote(
                pbuf.at[s], xrecv.at[j, p], x_send.at[0, 0], x_recv.at[j, p], mate
            ).wait_recv()
        pbuf[s] = pbuf[s] + ((xrecv[0, p] + xrecv[1, p]) + xrecv[2, p])
        return s

    p_mine = (zq + zh) % 2
    p_send = 1 - p_mine
    s_send = x_total(p_send)
    h_copy = remote(pbuf.at[s_send], zrecv, h_send, h_recv, hpeer)
    h_copy.start()
    s_mine = x_total(p_mine)
    h_copy.wait_recv()
    out[...] = (pbuf[s_mine] + zrecv[...]).T

    h_copy.wait_send()
    for c in z_copies(0):
        c.wait_send()
    for k in range(4):
        for c in y_copies(k):
            c.wait_send()
        for c in f_copies(k):
            c.wait_send()

    @pl.when(inner)
    def _():
        for c in z_copies(1):
            c.wait_send()
        for k in (1, 2, 3):
            for c in zf_copies(k):
                c.wait_send()

    for d in range(4):
        for p in range(2):
            c_copy(d, p, loop).wait_send()

        @pl.when(x != ys[d])
        def _():
            for p in range(2):
                x_copy(d, p).wait_send()


def ladder_of(amplitudes, integrals, screen_mask):
    dma = pltpu.SemaphoreType.DMA
    return pl.pallas_call(
        kernel,
        out_shape=jax.ShapeDtypeStruct((TILE, IC), F32),
        in_specs=[
            pl.BlockSpec(memory_space=pl.ANY),
            pl.BlockSpec(memory_space=pl.ANY),
            pl.BlockSpec(memory_space=pltpu.SMEM),
        ],
        out_specs=pl.BlockSpec(memory_space=pltpu.VMEM),
        scratch_shapes=[
            pltpu.VMEM((NL, 2, HALF, TILE), F32),
            pltpu.VMEM((CR, IC), F32),
            pltpu.VMEM((IC, CR), BF),
            pltpu.VMEM((IC, CR), BF),
            pltpu.VMEM((CR, 2 * TILE), BF),
            pltpu.VMEM((NL, IC, TILE), F32),
            pltpu.VMEM((8, IC, TILE), F32),
            pltpu.VMEM((3, 2, IC, TILE), F32),
            pltpu.VMEM((IC, TILE), F32),
            dma((2,)),
            dma((NL, 2)),
            dma((2, 4, 2)),
            dma((2, 4)),
            dma((2, 2)),
            dma((3, 2)),
            dma((8,)),
            dma((8,)),
            dma((4, 2)),
            dma((3, 2)),
            dma,
            dma,
        ],
        compiler_params=pltpu.CompilerParams(
            collective_id=0, has_side_effects=True, vmem_limit_bytes=60 * 1024 * 1024
        ),
        cost_estimate=pl.CostEstimate(
            flops=2 * 3 * CR * CR * IC, bytes_accessed=24 * 2**20, transcendentals=0
        ),
    )(amplitudes, integrals.reshape(2, HALF, TILE), screen_mask)


def on_device(amplitudes, integrals, screen_mask, base_residual, vir_energy, occ_energy):
    ladder = ladder_of(amplitudes, integrals, screen_mask)
    residual = base_residual + ladder
    update = residual / (vir_energy[:, None] + occ_energy[None, :])
    return (residual, update)


def solution(mesh):
    in_specs = (
        P("row", "loop"),
        P("row", "loop"),
        P("row", None),
        P("row", "loop"),
        P("row"),
        P("loop"),
    )
    out_specs = (P("row", "loop"), P("row", "loop"))
    return jax.shard_map(
        on_device, mesh=mesh, in_specs=in_specs, out_specs=out_specs, check_vma=False
    )
```

```python
import jax
import jax.numpy as jnp
from jax import lax
from jax.experimental import pallas as pl
from jax.experimental.pallas import tpu as pltpu
from jax.sharding import PartitionSpec as P

TILE = 128
NL = 16
CR = 2048
FIRST_Y = 336
NA = (CR - FIRST_Y) // 2
NB = FIRST_Y // 2
A0, A1, B0, B1, BB = (0, NA), (NA, NA), (2 * NA, NB), (2 * NA + NB, NB), (2 * NA, FIRST_Y)
SEM = {A0: 0, A1: 1, B0: 2, B1: 3, BB: 2}
TI = 256
NT = 3
IC = 768
BF = jnp.bfloat16
F32 = jnp.float32
MESH = pl.DeviceIdType.MESH


def kernel(
    amp_hbm,
    int_hbm,
    mask,
    out,
    blk,
    t32,
    tth,
    ttl,
    rhs,
    pbuf,
    crecv,
    xrecv,
    zrecv,
    load_sem,
    g_recv,
    y_send,
    yb_send,
    yf_send,
    z_send,
    zf_send,
    zb_send,
    zbf_send,
    c_send,
    c_recv,
    x_send,
    x_recv,
    h_send,
    h_recv,
):
    row = lax.axis_index("row")
    loop = lax.axis_index("loop")
    x, zh, core = row // 4, (row // 2) % 2, row % 2
    y, z = loop // 4, loop % 4
    zq = z // 2
    inner = ((z + 1) // 2) % 2 == 1
    ys = [y, (y + 1) % 4, (y + 3) % 4, (y + 2) % 4]
    zs = [z, z + 1 - 2 * (z % 2), 2 - zq, 3 - 3 * zq]

    def slot(d, k):
        return ys[d] * 4 + zs[k]

    up = (row, ys[1] * 4 + z)
    down = (row, ys[2] * 4 + z)
    znear = (row, y * 4 + zs[1])
    zfar = (row, y * 4 + 3 - z)
    mate = (row + 1 - 2 * core, loop)
    hpeer = (row + 2 - 4 * zh, loop)

    barrier = pltpu.get_barrier_semaphore()
    peers = [up, down, znear, mate, hpeer]
    peers += [(((x + j) % 4) * 4 + zh * 2 + core, loop) for j in (1, 2, 3)]
    for peer in peers:
        pl.semaphore_signal(barrier, inc=1, device_id=peer, device_id_type=MESH)

    @pl.when(inner)
    def _():
        pl.semaphore_signal(barrier, inc=1, device_id=zfar, device_id_type=MESH)

    load_t = pltpu.make_async_copy(amp_hbm, t32, load_sem.at[0])
    load_t.start()
    load_b = pltpu.make_async_copy(int_hbm, blk.at[loop], load_sem.at[1])
    load_b.start()
    pl.semaphore_wait(barrier, len(peers) + ((z + 1) // 2) % 2)

    def remote(src, dst, send, recv, to):
        return pltpu.make_async_remote_copy(
            src_ref=src,
            dst_ref=dst,
            send_sem=send,
            recv_sem=recv,
            device_id=to,
            device_id_type=MESH,
        )

    def g_copy(s, part, send, to, own=False):
        view = pl.ds(part[0], part[1])
        src = int_hbm.at[view] if own else blk.at[s, view]
        return remote(src, blk.at[s, view], send, g_recv.at[s, SEM[part]], to)

    def arrived(d, k, part):
        g_copy(slot(d, k), part, y_send.at[0, 0, 0], up).wait_recv()

    def y_copies(k):
        s = slot(0, k)
        own = k == 0
        return [
            g_copy(s, A0, y_send.at[0, k, 0], up, own),
            g_copy(s, A1, y_send.at[1, k, 1], down, own),
            g_copy(s, A1, y_send.at[0, k, 1], up, own),
            g_copy(s, A0, y_send.at[1, k, 0], down, own),
        ]

    def yb_copies():
        return [g_copy(loop, BB, yb_send.at[n], to, True) for n, to in enumerate((up, down))]

    def zf_copies(k):
        s = slot(0, k)
        to = znear if k > 1 else zfar
        return [g_copy(s, h, zf_send.at[k - 1, n], to) for n, h in enumerate((A0, A1))]

    def z_copies(far):
        to = zfar if far else znear
        return [g_copy(loop, h, z_send.at[far, n], to, True) for n, h in enumerate((A0, A1))]

    def zb_copies(far):
        to = zfar if far else znear
        return [g_copy(slot(d, 0), BB, zb_send.at[far, d], to) for d in range(4)]

    def zbf_copies(k):
        to = znear if k > 1 else zfar
        return [g_copy(slot(d, k), BB, zbf_send.at[k - 1, d], to) for d in range(4)]

    def f_copies(k):
        return [
            g_copy(slot(2, k), A0, yf_send.at[0, k], up),
            g_copy(slot(1, k), A1, yf_send.at[1, k], down),
        ]

    def fb_copies():
        return [
            g_copy(slot(2, 0), B0, yf_send.at[0, 4], up),
            g_copy(slot(1, 0), B1, yf_send.at[1, 4], down),
        ]

    for c in z_copies(0):
        c.start()

    @pl.when(inner)
    def _():
        for c in z_copies(1):
            c.start()

    for c in yb_copies() + y_copies(0):
        c.start()

    load_t.wait()

    def prep(j, carry):
        at = pl.multiple_of(j * 128, 128)
        t = t32[pl.ds(at, 128), :].T
        hi = t.astype(BF)
        tth[:, pl.ds(at, 128)] = hi
        ttl[:, pl.ds(at, 128)] = (t - hi.astype(F32)).astype(BF)
        return carry

    lax.fori_loop(0, CR // 128, prep, 0)

    def split(s):
        def body(j, carry):
            at = pl.multiple_of(j * 128, 128)
            m = blk[s, pl.ds(at, 128), :] * mask[j, s].astype(F32)
            hi = m.astype(BF)
            rhs[pl.ds(at, 128), 0:128] = hi
            rhs[pl.ds(at, 128), 128:256] = (m - hi.astype(F32)).astype(BF)
            return carry

        lax.fori_loop(0, CR // 128, body, 0)

    def multiply(s, j):
        at = pl.ds(pl.multiple_of(j * TI, TI), TI)
        a = jnp.dot(tth[at, :], rhs[...], preferred_element_type=F32)
        b = jnp.dot(ttl[at, :], rhs[:, 0:128], preferred_element_type=F32)
        pbuf[s, at, :] = a[:, 0:128] + (a[:, 128:256] + b)

    def tile(j):
        return pl.ds(j * TI, TI)

    def c_copy(d, k, j):
        n = d * 2 + k // 2
        return remote(
            pbuf.at[slot(d, k), tile(j)],
            crecv.at[n, tile(j)],
            c_send.at[n, j],
            c_recv.at[n, j],
            mate,
        )

    def keeps(k):
        return (zs[k] + core) % 2 == 0

    def x_copy(d, p, s, j):
        yv = ys[d]
        place = (x + 4 - yv) % 4 - 1
        to = (yv * 4 + zh * 2 + core, loop)
        return remote(
            pbuf.at[s, tile(j)],
            xrecv.at[place, p, tile(j)],
            x_send.at[d, p, j],
            x_recv.at[place, p, j],
            to,
        )

    def to_mate(d, k, j):
        @pl.when(jnp.logical_not(keeps(k)))
        def _():
            c_copy(d, k, j).start()

    def reduce(d, k, j):
        @pl.when(keeps(k))
        def _():
            n = d * 2 + k // 2
            s = slot(d, k)
            c_copy(d, k, j).wait_recv()
            pbuf[s, tile(j)] = pbuf[s, tile(j)] + crecv[n, tile(j)]

            @pl.when(x != ys[d])
            def _():
                x_copy(d, k // 2, s, j).start()

    def compute(d, k):
        s = slot(d, k)
        split(s)

        def body(j, carry):
            multiply(s, j)
            return carry

        lax.fori_loop(0, NT, body, 0)
        for j in range(NT):
            to_mate(d, k, j)

    def reduce_all(d, k):
        for j in range(NT):
            reduce(d, k, j)

    def y_out(k):
        for c in y_copies(k):
            c.start()

    def z_forward(k):
        for part in (A0, A1):
            arrived(0, k, part)

        @pl.when(inner)
        def _():
            for c in zf_copies(k):
                c.start()

    def zb_forward(k):
        for d in range(4):
            arrived(d, k, BB)

        @pl.when(inner)
        def _():
            for c in zbf_copies(k):
                c.start()

    def y_forward(k):
        up_c, down_c = f_copies(k)
        arrived(2, k, A0)
        up_c.start()
        arrived(1, k, A1)
        down_c.start()

    def rest(k):
        arrived(1, k, A0)
        arrived(2, k, A1)

    def last(k):
        arrived(3, k, A0)
        arrived(3, k, A1)

    def x_total(p):
        s = x * 4 + 2 * ((zq + p) % 2) + core
        for j in range(NT):
            for i in range(3):
                remote(
                    pbuf.at[s, tile(j)],
                    xrecv.at[i, p, tile(j)],
                    x_send.at[0, 0, 0],
                    x_recv.at[i, p, j],
                    mate,
                ).wait_recv()
            pbuf[s, tile(j)] = pbuf[s, tile(j)] + (
                (xrecv[0, p, tile(j)] + xrecv[1, p, tile(j)]) + xrecv[2, p, tile(j)]
            )

            @pl.when((zq + zh + p) % 2 == 1)
            def _():
                h_copy(s, j).start()

    def h_copy(s, j):
        return remote(
            pbuf.at[s, tile(j)], zrecv.at[tile(j)], h_send.at[j], h_recv.at[j], hpeer
        )

    up_b, down_b = fb_copies()
    arrived(2, 0, BB)
    up_b.start()
    arrived(1, 0, BB)
    down_b.start()
    load_b.wait()
    compute(0, 0)
    z_forward(1)
    y_out(1)
    arrived(3, 0, B0)
    arrived(3, 0, B1)
    for c in zb_copies(0):
        c.start()

    @pl.when(inner)
    def _():
        for c in zb_copies(1):
            c.start()

    y_forward(0)
    rest(0)
    compute(1, 0)
    compute(2, 0)
    z_forward(2)
    y_out(2)
    y_forward(1)
    rest(1)
    last(0)
    compute(3, 0)
    zb_forward(1)
    compute(0, 1)
    reduce_all(0, 0)
    reduce_all(0, 1)
    z_forward(3)
    y_out(3)
    compute(1, 1)
    reduce_all(1, 0)
    reduce_all(1, 1)
    compute(2, 1)
    reduce_all(2, 0)
    reduce_all(2, 1)
    y_forward(2)
    rest(2)
    zb_forward(2)
    compute(0, 2)
    compute(1, 2)
    last(1)
    compute(3, 1)
    reduce_all(3, 0)
    reduce_all(3, 1)
    compute(2, 2)
    zb_forward(3)
    y_forward(3)
    rest(3)
    compute(0, 3)
    reduce_all(0, 2)
    reduce_all(0, 3)
    compute(1, 3)
    reduce_all(1, 2)
    reduce_all(1, 3)
    compute(2, 3)
    reduce_all(2, 2)
    reduce_all(2, 3)
    x_total(0)
    last(2)
    compute(3, 2)
    reduce_all(3, 2)
    last(3)
    s_last = slot(3, 3)
    split(s_last)
    multiply(s_last, 0)
    to_mate(3, 3, 0)
    multiply(s_last, 1)
    to_mate(3, 3, 1)
    reduce(3, 3, 0)
    multiply(s_last, 2)
    to_mate(3, 3, 2)
    reduce(3, 3, 1)
    reduce(3, 3, 2)
    x_total(1)
    s_mine = x * 4 + 2 * zh + core
    for j in range(NT):
        h_copy(s_mine, j).wait_recv()
        out[:, j * TI : (j + 1) * TI] = (pbuf[s_mine, tile(j)] + zrecv[tile(j)]).T

    for j in range(NT):
        h_copy(s_mine, j).wait_send()
    for c in z_copies(0) + yb_copies() + fb_copies() + zb_copies(0):
        c.wait_send()
    for k in range(4):
        for c in y_copies(k) + f_copies(k):
            c.wait_send()

    @pl.when(inner)
    def _():
        for c in z_copies(1) + zb_copies(1):
            c.wait_send()
        for k in (1, 2, 3):
            for c in zf_copies(k) + zbf_copies(k):
                c.wait_send()

    for d in range(4):
        for p in range(2):
            for j in range(NT):
                c_copy(d, 2 * p, j).wait_send()

        @pl.when(x != ys[d])
        def _():
            for p in range(2):
                for j in range(NT):
                    x_copy(d, p, loop, j).wait_send()


def ladder_of(amplitudes, integrals, screen_mask):
    dma = pltpu.SemaphoreType.DMA
    return pl.pallas_call(
        kernel,
        out_shape=jax.ShapeDtypeStruct((TILE, IC), F32),
        in_specs=[
            pl.BlockSpec(memory_space=pl.ANY),
            pl.BlockSpec(memory_space=pl.ANY),
            pl.BlockSpec(memory_space=pltpu.SMEM),
        ],
        out_specs=pl.BlockSpec(memory_space=pltpu.VMEM),
        scratch_shapes=[
            pltpu.VMEM((NL, CR, TILE), F32),
            pltpu.VMEM((CR, IC), F32),
            pltpu.VMEM((IC, CR), BF),
            pltpu.VMEM((IC, CR), BF),
            pltpu.VMEM((CR, 2 * TILE), BF),
            pltpu.VMEM((NL, IC, TILE), F32),
            pltpu.VMEM((8, IC, TILE), F32),
            pltpu.VMEM((3, 2, IC, TILE), F32),
            pltpu.VMEM((IC, TILE), F32),
            dma((2,)),
            dma((NL, 4)),
            dma((2, 4, 2)),
            dma((2,)),
            dma((2, 5)),
            dma((2, 2)),
            dma((3, 2)),
            dma((2, 4)),
            dma((3, 4)),
            dma((8, NT)),
            dma((8, NT)),
            dma((4, 2, NT)),
            dma((3, 2, NT)),
            dma((NT,)),
            dma((NT,)),
        ],
        compiler_params=pltpu.CompilerParams(
            collective_id=0, has_side_effects=True, vmem_limit_bytes=60 * 1024 * 1024
        ),
        cost_estimate=pl.CostEstimate(
            flops=2 * 3 * CR * CR * IC, bytes_accessed=24 * 2**20, transcendentals=0
        ),
    )(amplitudes, integrals, screen_mask)


def on_device(amplitudes, integrals, screen_mask, base_residual, vir_energy, occ_energy):
    ladder = ladder_of(amplitudes, integrals, screen_mask)
    residual = base_residual + ladder
    update = residual / (vir_energy[:, None] + occ_energy[None, :])
    return (residual, update)


def solution(mesh):
    in_specs = (
        P("row", "loop"),
        P("row", "loop"),
        P("row", None),
        P("row", "loop"),
        P("row"),
        P("loop"),
    )
    out_specs = (P("row", "loop"), P("row", "loop"))
    return jax.shard_map(
        on_device, mesh=mesh, in_specs=in_specs, out_specs=out_specs, check_vma=False
    )
```

```python
import jax
import jax.numpy as jnp
from jax import lax
from jax.experimental import pallas as pl
from jax.experimental.pallas import tpu as pltpu
from jax.sharding import PartitionSpec as P

TILE = 128
NL = 16
CR = 2048
HR = CR // 2
IC = 768
TI = 256
NT = IC // TI
BF = jnp.bfloat16
F32 = jnp.float32
MESH = pl.DeviceIdType.MESH

ORDER = [
    ("own",),
    ("prep",),
    ("block", 0, 0),
    ("own_second",),
    ("z_pass", 0, 1),
    ("z_pass", 0, 2),
    ("y_out", 0, 1),
    ("block", 1, 0),
    ("block", 2, 0),
    ("block", 0, 1),
    ("z_pass", 1, 1),
    ("z_pass", 1, 2),
    ("y_out", 1, 1),
    ("block", 3, 0),
    ("block", 1, 1),
    ("sum", 0, (0, 1), (0, 1), (0, 1, 2)),
    ("amp", 0),
    ("part", 0, 0, 0, 4),
    ("part", 1, 0, 0, 2),
    ("z_pass", 0, 3),
    ("y_out", 0, 2),
    ("block", 0, 2),
    ("block", 2, 1),
    ("z_pass", 1, 3),
    ("y_out", 1, 2),
    ("block", 1, 2),
    ("block", 3, 1),
    ("sum", 0, (2, 3), (0, 1), (0, 1, 2)),
    ("part", 1, 0, 2, 4),
    ("part", 2, 0, 0, 2),
    ("sum", 1, (0, 1, 2, 3), (0, 1), (0,)),
    ("amp", 1),
    ("y_out", 0, 3),
    ("part", 0, 1, 0, 4),
    ("part", 1, 1, 0, 4),
    ("part", 2, 1, 0, 2),
    ("block", 0, 3),
    ("block", 2, 2),
    ("sum", 1, (0, 1, 2, 3), (0, 1), (1,)),
    ("y_out", 1, 3),
    ("block", 1, 3),
    ("block", 3, 2),
    ("sum", 0, (0, 1), (2, 3), (0, 1, 2)),
    ("part", 2, 0, 2, 4),
    ("part", 2, 1, 2, 4),
    ("part", 3, 0, 0, 2),
    ("part", 3, 1, 0, 2),
    ("sum", 1, (0, 1), (2, 3), (0, 1)),
    ("amp", 2),
    ("part", 0, 2, 0, 4),
    ("part", 1, 2, 0, 4),
    ("sum", 1, (0, 1, 2, 3), (0, 1), (2,)),
    ("block", 2, 3),
    ("part", 2, 2, 0, 4),
    ("part", 3, 2, 0, 2),
    ("sum", 1, (0, 1), (2, 3), (2,)),
    ("part", 3, 0, 2, 3),
    ("part", 3, 1, 2, 3),
    ("part", 3, 2, 2, 3),
    ("total", 1, 0),
    ("sum", 1, (2,), (2, 3), (0, 1, 2)),
    ("sum", 0, (2,), (2, 3), (0, 1, 2)),
    ("sum", 1, (3,), (2,), (0, 1, 2)),
    ("sum", 0, (3,), (2,), (0, 1, 2)),
    ("total", 0, 0),
    ("last",),
    ("total", 1, 1),
    ("total", 0, 1),
]


def kernel(
    amp_hbm,
    int_hbm,
    mask,
    out,
    blk,
    t32,
    tp32,
    tth,
    ttl,
    rhs,
    pbuf,
    crecv,
    xrecv,
    srecv,
    zrecv,
    load_sem,
    g_recv,
    o_send,
    a_send,
    a_recv,
    y_send,
    z_send,
    zf_send,
    c_send,
    c_recv,
    x_send,
    x_recv,
    s_send,
    s_recv,
    h_send,
    h_recv,
):
    row = lax.axis_index("row")
    loop = lax.axis_index("loop")
    x, zh, core = row // 4, (row // 2) % 2, row % 2
    y, z = loop // 4, loop % 4
    half = y // 2
    zq = z // 2
    inner = ((z + 1) // 2) % 2 == 1
    zs = [z, z + 1 - 2 * (z % 2), 2 - zq, 3 - 3 * zq]

    def y_of(d):
        base = y + (d % 2) * (3 - 2 * y)
        return base + (d // 2) * (1 - 2 * (base % 2))

    def slot(d, k):
        return y_of(d) * 4 + zs[k]

    partner = (row, (3 - y) * 4 + z)
    ymate = (row, y_of(2) * 4 + z)
    znear = (row, y * 4 + zs[1])
    zfar = (row, y * 4 + 3 - z)
    mate = (row + 1 - 2 * core, loop)
    hpeer = (row + 2 - 4 * zh, loop)
    mine = pl.ds(pl.multiple_of(half * HR, HR), HR)
    theirs = pl.ds(pl.multiple_of((1 - half) * HR, HR), HR)

    barrier = pltpu.get_barrier_semaphore()
    peers = [partner, ymate, znear, mate, hpeer]
    peers += [(((x + j) % 4) * 4 + zh * 2 + core, loop) for j in (1, 2, 3)]
    for peer in peers:
        pl.semaphore_signal(barrier, inc=1, device_id=peer, device_id_type=MESH)

    @pl.when(inner)
    def _():
        pl.semaphore_signal(barrier, inc=1, device_id=zfar, device_id_type=MESH)

    load_b = pltpu.make_async_copy(int_hbm.at[mine], blk.at[loop], load_sem.at[1])
    load_b.start()
    load_t = pltpu.make_async_copy(amp_hbm.at[mine], t32, load_sem.at[0])
    load_t.start()
    pl.semaphore_wait(barrier, len(peers) + ((z + 1) // 2) % 2)

    def remote(src, dst, send, recv, to):
        return pltpu.make_async_remote_copy(
            src_ref=src,
            dst_ref=dst,
            send_sem=send,
            recv_sem=recv,
            device_id=to,
            device_id_type=MESH,
        )

    def tile(j):
        return pl.ds(j * TI, TI)

    def g_copy(d, k, send, to):
        s = slot(d, k)
        src = int_hbm.at[mine] if (d, k) == (0, 0) else blk.at[s]
        return remote(src, blk.at[s], send, g_recv.at[s], to)

    def half_copy():
        return remote(int_hbm.at[theirs], blk.at[loop], o_send, g_recv.at[loop], partner)

    def amp_copy(j):
        return remote(
            amp_hbm.at[theirs, tile(j)], tp32.at[j], a_send.at[j], a_recv.at[j], partner
        )

    def y_copy(d, k):
        return g_copy(d, k, y_send.at[d, k], ymate)

    def z_copy(d, far):
        return g_copy(d, 0, z_send.at[d, far], zfar if far else znear)

    def zf_copy(d, k):
        return g_copy(d, k, zf_send.at[d, k - 1], znear if k > 1 else zfar)

    def arrived(d, k):
        s = slot(d, k)
        remote(blk.at[s], blk.at[s], o_send, g_recv.at[s], partner).wait_recv()

    seen = {True: set(), False: set()}

    def need(d, k):
        if (d, k) == (0, 0):
            return
        todo = [where for where in seen if (d, k) not in seen[where]]
        for where in todo:
            seen[where].add((d, k))
        if len(todo) == 2:
            arrived(d, k)
        elif todo:

            @pl.when(inner if todo[0] else jnp.logical_not(inner))
            def _():
                arrived(d, k)

    def z_out(d):
        z_copy(d, 0).start()

        @pl.when(inner)
        def _():
            z_copy(d, 1).start()

    def own():
        half_copy().start()
        y_copy(0, 0).start()
        z_out(0)
        for j in range(NT):
            amp_copy(j).start()

    def own_second():
        need(1, 0)
        z_out(1)
        y_copy(1, 0).start()

    def z_pass(d, k):
        @pl.when(inner)
        def _():
            arrived(d, k)
            zf_copy(d, k).start()

        seen[True].add((d, k))

    def y_out(d, k):
        need(d, k)
        y_copy(d, k).start()

    def put_amp(q, rows, at, t):
        hi = t.astype(BF)
        tth[q, rows, pl.ds(at, 128)] = hi
        ttl[q, rows, pl.ds(at, 128)] = (t - hi.astype(F32)).astype(BF)

    def prep():
        load_t.wait()

        def body(i, carry):
            at = pl.multiple_of(i * 128, 128)
            put_amp(0, pl.ds(0, IC), at, t32[pl.ds(at, 128), :].T)
            return carry

        lax.fori_loop(0, HR // 128, body, 0)

    def amp(j):
        amp_copy(j).wait_recv()

        def body(i, carry):
            at = pl.multiple_of(i * 128, 128)
            put_amp(1, tile(j), at, tp32[j, pl.ds(at, 128), :].T)
            return carry

        lax.fori_loop(0, HR // 128, body, 0)

    def split(s):
        def body(i, carry):
            at = pl.multiple_of(i * 128, 128)
            m = blk[s, pl.ds(at, 128), :] * mask[half * (HR // 128) + i, s].astype(F32)
            hi = m.astype(BF)
            rhs[s, pl.ds(at, 128), 0:128] = hi
            rhs[s, pl.ds(at, 128), 128:256] = (m - hi.astype(F32)).astype(BF)
            return carry

        lax.fori_loop(0, HR // 128, body, 0)

    def multiply(q, s, j):
        at = pl.ds(pl.multiple_of(j * TI, TI), TI)
        a = jnp.dot(tth[q, at, :], rhs[s], preferred_element_type=F32)
        b = jnp.dot(ttl[q, at, :], rhs[s, :, 0:128], preferred_element_type=F32)
        pbuf[q, s, at, :] = a[:, 0:128] + (a[:, 128:256] + b)

    def keeps(k):
        return (zs[k] + core) % 2 == 0

    def c_copy(q, d, k, j):
        n = d * 2 + k // 2
        return remote(
            pbuf.at[q, slot(d, k), tile(j)],
            crecv.at[q, n, tile(j)],
            c_send.at[q, n, j],
            c_recv.at[q, n, j],
            mate,
        )

    def x_copy(q, d, p, s, j):
        yv = y_of(d)
        place = (x + 4 - yv) % 4 - 1
        to = (yv * 4 + zh * 2 + core, loop)
        return remote(
            pbuf.at[q, s, tile(j)],
            xrecv.at[q, place, p, tile(j)],
            x_send.at[q, d, p, j],
            x_recv.at[q, place, p, j],
            to,
        )

    def to_mate(q, d, k, j):
        @pl.when(jnp.logical_not(keeps(k)))
        def _():
            c_copy(q, d, k, j).start()

    def reduce(q, d, k, j):
        @pl.when(keeps(k))
        def _():
            n = d * 2 + k // 2
            s = slot(d, k)
            c_copy(q, d, k, j).wait_recv()
            pbuf[q, s, tile(j)] = pbuf[q, s, tile(j)] + crecv[q, n, tile(j)]

            @pl.when(x != y_of(d))
            def _():
                x_copy(q, d, k // 2, s, j).start()

    def ready(d, k):
        if (d, k) == (0, 0):
            load_b.wait()
        need(d, k)
        s = slot(d, k)
        split(s)
        return s

    def block(d, k):
        s = ready(d, k)

        def body(j, carry):
            multiply(0, s, j)
            return carry

        lax.fori_loop(0, NT, body, 0)
        for j in range(NT):
            to_mate(0, d, k, j)

    def part(k, j, low, high):
        def body(d, carry):
            multiply(1, slot(d, k), j)
            to_mate(1, d, k, j)
            return carry

        lax.fori_loop(low, high, body, 0)

    def sums(q, ds, ks, js):
        for d in ds:
            for k in ks:
                for j in js:
                    reduce(q, d, k, j)

    def last():
        s = ready(3, 3)
        todo = [(1, 0), (1, 1), (1, 2), (0, 0), (0, 1), (0, 2)]
        for n, (q, j) in enumerate(todo):
            multiply(q, s, j)
            to_mate(q, 3, 3, j)
            if n:
                reduce(todo[n - 1][0], 3, 3, todo[n - 1][1])
        reduce(0, 3, 3, NT - 1)

    def h_copy(s, j):
        return remote(
            pbuf.at[0, s, tile(j)], zrecv.at[tile(j)], h_send.at[j], h_recv.at[j], hpeer
        )

    def s_copy(p, s, j):
        return remote(
            pbuf.at[1, s, tile(j)],
            srecv.at[p, tile(j)],
            s_send.at[p, j],
            s_recv.at[p, j],
            partner,
        )

    def total(q, p):
        s = x * 4 + 2 * ((zq + p) % 2) + core
        for j in range(NT):
            for i in range(3):
                dst = xrecv.at[q, i, p, tile(j)]
                remote(dst, dst, o_send, x_recv.at[q, i, p, j], partner).wait_recv()
            add = (xrecv[q, 0, p, tile(j)] + xrecv[q, 1, p, tile(j)]) + xrecv[
                q, 2, p, tile(j)
            ]
            if q == 1:
                pbuf[1, s, tile(j)] = pbuf[1, s, tile(j)] + add
                s_copy(p, s, j).start()
            else:
                s_copy(p, s, j).wait_recv()
                pbuf[0, s, tile(j)] = (pbuf[0, s, tile(j)] + add) + srecv[p, tile(j)]

                @pl.when((zq + zh + p) % 2 == 1)
                def _():
                    h_copy(s, j).start()

    steps = {
        "own": own,
        "own_second": own_second,
        "z_pass": z_pass,
        "y_out": y_out,
        "prep": prep,
        "amp": amp,
        "block": block,
        "part": part,
        "last": last,
        "sum": sums,
        "total": total,
    }
    for name, *where in ORDER:
        steps[name](*where)
    s_mine = x * 4 + 2 * zh + core
    for j in range(NT):
        h_copy(s_mine, j).wait_recv()
        out[:, j * TI : (j + 1) * TI] = (pbuf[0, s_mine, tile(j)] + zrecv[tile(j)]).T

    sent = [half_copy(), z_copy(0, 0), z_copy(1, 0)]
    for j in range(NT):
        sent += [h_copy(s_mine, j), amp_copy(j)]
        sent += [s_copy(p, s_mine, j) for p in range(2)]
        sent += [c_copy(q, d, 2 * p, j) for q in (0, 1) for d in range(4) for p in (0, 1)]
    sent += [y_copy(d, k) for d in (0, 1) for k in range(4)]
    for c in sent:
        c.wait_send()

    @pl.when(inner)
    def _():
        for d in (0, 1):
            z_copy(d, 1).wait_send()
            for k in (1, 2, 3):
                zf_copy(d, k).wait_send()

    for d in range(4):

        @pl.when(x != y_of(d))
        def _():
            for q in (0, 1):
                for p in (0, 1):
                    for j in range(NT):
                        x_copy(q, d, p, loop, j).wait_send()


def ladder_of(amplitudes, integrals, screen_mask):
    dma = pltpu.SemaphoreType.DMA
    return pl.pallas_call(
        kernel,
        out_shape=jax.ShapeDtypeStruct((TILE, IC), F32),
        in_specs=[
            pl.BlockSpec(memory_space=pl.ANY),
            pl.BlockSpec(memory_space=pl.ANY),
            pl.BlockSpec(memory_space=pltpu.SMEM),
        ],
        out_specs=pl.BlockSpec(memory_space=pltpu.VMEM),
        scratch_shapes=[
            pltpu.VMEM((NL, HR, TILE), F32),
            pltpu.VMEM((HR, IC), F32),
            pltpu.VMEM((NT, HR, TI), F32),
            pltpu.VMEM((2, IC, HR), BF),
            pltpu.VMEM((2, IC, HR), BF),
            pltpu.VMEM((NL, HR, 2 * TILE), BF),
            pltpu.VMEM((2, NL, IC, TILE), F32),
            pltpu.VMEM((2, 8, IC, TILE), F32),
            pltpu.VMEM((2, 3, 2, IC, TILE), F32),
            pltpu.VMEM((2, IC, TILE), F32),
            pltpu.VMEM((IC, TILE), F32),
            dma((2,)),
            dma((NL,)),
            dma,
            dma((NT,)),
            dma((NT,)),
            dma((2, 4)),
            dma((2, 2)),
            dma((2, 3)),
            dma((2, 8, NT)),
            dma((2, 8, NT)),
            dma((2, 4, 2, NT)),
            dma((2, 3, 2, NT)),
            dma((2, NT)),
            dma((2, NT)),
            dma((NT,)),
            dma((NT,)),
        ],
        compiler_params=pltpu.CompilerParams(
            collective_id=0, has_side_effects=True, vmem_limit_bytes=60 * 1024 * 1024
        ),
        cost_estimate=pl.CostEstimate(
            flops=2 * 3 * CR * CR * IC, bytes_accessed=24 * 2**20, transcendentals=0
        ),
    )(amplitudes, integrals, screen_mask)


def on_device(amplitudes, integrals, screen_mask, base_residual, vir_energy, occ_energy):
    ladder = ladder_of(amplitudes, integrals, screen_mask)
    residual = base_residual + ladder
    update = residual / (vir_energy[:, None] + occ_energy[None, :])
    return (residual, update)


def solution(mesh):
    in_specs = (
        P("row", "loop"),
        P("row", "loop"),
        P("row", None),
        P("row", "loop"),
        P("row"),
        P("loop"),
    )
    out_specs = (P("row", "loop"), P("row", "loop"))
    return jax.shard_map(
        on_device, mesh=mesh, in_specs=in_specs, out_specs=out_specs, check_vma=False
    )
```

```python
import jax
import jax.numpy as jnp
from jax import lax
from jax.experimental import pallas as pl
from jax.experimental.pallas import tpu as pltpu
from jax.sharding import PartitionSpec as P

TILE = 128
NL = 16
CR = 2048
HR = CR // 2
IC = 768
TI = 256
NT = IC // TI
BF = jnp.bfloat16
F32 = jnp.float32
MESH = pl.DeviceIdType.MESH

ORDER = [
    ("own",),
    ("prep",),
    ("block", 0, 0),
    ("own_second",),
    ("z_pass", 0, 1),
    ("z_pass", 0, 2),
    ("y_out", 0, 1),
    ("block", 1, 0),
    ("sum", 0, (0,), (0,), (0, 1, 2)),
    ("block", 2, 0),
    ("sum", 0, (1,), (0,), (0, 1, 2)),
    ("block", 0, 1),
    ("sum", 0, (2,), (0,), (0, 1, 2)),
    ("z_pass", 1, 1),
    ("z_pass", 1, 2),
    ("y_out", 1, 1),
    ("block", 3, 0),
    ("sum", 0, (0,), (1,), (0, 1, 2)),
    ("block", 1, 1),
    ("sum", 0, (3,), (0,), (0, 1, 2)),
    ("sum", 0, (1,), (1,), (0, 1, 2)),
    ("amp", 0),
    ("part", 0, 0, 0, 4),
    ("part", 1, 0, 0, 2),
    ("z_pass", 0, 3),
    ("y_out", 0, 2),
    ("sum", 1, (2, 3, 0, 1), (0,), (0,)),
    ("sum", 1, (0, 1), (1,), (0,)),
    ("block", 0, 2),
    ("block", 2, 1),
    ("sum", 0, (0,), (2,), (0, 1, 2)),
    ("sum", 0, (2,), (1,), (0, 1, 2)),
    ("z_pass", 1, 3),
    ("y_out", 1, 2),
    ("block", 3, 1),
    ("block", 1, 2),
    ("sum", 0, (3,), (1,), (0, 1, 2)),
    ("sum", 0, (1,), (2,), (0, 1, 2)),
    ("part", 1, 0, 2, 4),
    ("part", 2, 0, 0, 2),
    ("sum", 1, (2, 3), (1,), (0,)),
    ("sum", 1, (0, 1), (2,), (0,)),
    ("amp", 1),
    ("y_out", 0, 3),
    ("part", 0, 1, 0, 4),
    ("part", 1, 1, 0, 4),
    ("sum", 1, (2, 3, 0, 1), (0, 1), (1,)),
    ("block", 2, 2),
    ("block", 0, 3),
    ("sum", 0, (2,), (2,), (0, 1, 2)),
    ("sum", 0, (0,), (3,), (0, 1, 2)),
    ("part", 2, 1, 0, 3),
    ("part", 2, 0, 2, 3),
    ("part", 3, 0, 0, 1),
    ("part", 3, 1, 0, 1),
    ("sum", 1, (2,), (2,), (0, 1)),
    ("sum", 1, (0, 1), (2,), (1,)),
    ("sum", 1, (0,), (3,), (0, 1)),
    ("y_out", 1, 3),
    ("block", 3, 2),
    ("block", 1, 3),
    ("sum", 0, (3,), (2,), (0, 1, 2)),
    ("sum", 0, (1,), (3,), (0, 1, 2)),
    ("part", 2, 0, 3, 4),
    ("part", 2, 1, 3, 4),
    ("sum", 1, (3,), (2,), (0, 1)),
    ("part", 3, 0, 1, 2),
    ("part", 3, 1, 1, 2),
    ("sum", 1, (1,), (3,), (0, 1)),
    ("amp", 2),
    ("part", 0, 2, 0, 4),
    ("part", 1, 2, 0, 4),
    ("sum", 1, (2, 3, 0, 1), (0, 1), (2,)),
    ("block", 2, 3),
    ("part", 2, 2, 0, 4),
    ("sum", 0, (2,), (3,), (0, 1, 2)),
    ("sum", 1, (2, 3, 0, 1), (2,), (2,)),
    ("part", 3, 2, 0, 3),
    ("part", 3, 0, 2, 3),
    ("part", 3, 1, 2, 3),
    ("sum", 1, (2,), (3,), (0, 1, 2)),
    ("sum", 1, (0, 1), (3,), (2,)),
    ("last",),
    ("total", 1, 0),
    ("total", 0, 0),
    ("total", 1, 1),
    ("total", 0, 1),
]


def kernel(
    amp_hbm,
    int_hbm,
    mask,
    out,
    blk,
    t32,
    tp32,
    tth,
    ttl,
    rhs,
    pbuf,
    crecv,
    xrecv,
    srecv,
    zrecv,
    load_sem,
    g_recv,
    o_send,
    a_send,
    a_recv,
    y_send,
    z_send,
    zf_send,
    c_send,
    c_recv,
    x_send,
    x_recv,
    s_send,
    s_recv,
    h_send,
    h_recv,
):
    row = lax.axis_index("row")
    loop = lax.axis_index("loop")
    x, zh, core = row // 4, (row // 2) % 2, row % 2
    y, z = loop // 4, loop % 4
    half = y // 2
    zq = z // 2
    inner = ((z + 1) // 2) % 2 == 1
    zs = [z, z + 1 - 2 * (z % 2), 2 - zq, 3 - 3 * zq]

    def y_of(d):
        base = y + (d % 2) * (3 - 2 * y)
        return base + (d // 2) * (1 - 2 * (base % 2))

    def slot(d, k):
        return y_of(d) * 4 + zs[k]

    partner = (row, (3 - y) * 4 + z)
    ymate = (row, y_of(2) * 4 + z)
    znear = (row, y * 4 + zs[1])
    zfar = (row, y * 4 + 3 - z)
    mate = (row + 1 - 2 * core, loop)
    hpeer = (row + 2 - 4 * zh, loop)
    mine = pl.ds(pl.multiple_of(half * HR, HR), HR)
    theirs = pl.ds(pl.multiple_of((1 - half) * HR, HR), HR)

    barrier = pltpu.get_barrier_semaphore()
    peers = [partner, ymate, znear, mate, hpeer]
    peers += [(((x + j) % 4) * 4 + zh * 2 + core, loop) for j in (1, 2, 3)]
    for peer in peers:
        pl.semaphore_signal(barrier, inc=1, device_id=peer, device_id_type=MESH)

    @pl.when(inner)
    def _():
        pl.semaphore_signal(barrier, inc=1, device_id=zfar, device_id_type=MESH)

    load_b = pltpu.make_async_copy(int_hbm.at[mine], blk.at[loop], load_sem.at[1])
    load_b.start()
    load_t = pltpu.make_async_copy(amp_hbm.at[mine], t32, load_sem.at[0])
    load_t.start()
    pl.semaphore_wait(barrier, len(peers) + ((z + 1) // 2) % 2)

    def remote(src, dst, send, recv, to):
        return pltpu.make_async_remote_copy(
            src_ref=src,
            dst_ref=dst,
            send_sem=send,
            recv_sem=recv,
            device_id=to,
            device_id_type=MESH,
        )

    def tile(j):
        return pl.ds(j * TI, TI)

    def g_copy(d, k, send, to):
        s = slot(d, k)
        src = int_hbm.at[mine] if (d, k) == (0, 0) else blk.at[s]
        return remote(src, blk.at[s], send, g_recv.at[s], to)

    def half_copy():
        return remote(int_hbm.at[theirs], blk.at[loop], o_send, g_recv.at[loop], partner)

    def amp_copy(j):
        return remote(
            amp_hbm.at[theirs, tile(j)], tp32.at[j], a_send.at[j], a_recv.at[j], partner
        )

    def y_copy(d, k):
        return g_copy(d, k, y_send.at[d, k], ymate)

    def z_copy(d, far):
        return g_copy(d, 0, z_send.at[d, far], zfar if far else znear)

    def zf_copy(d, k):
        return g_copy(d, k, zf_send.at[d, k - 1], znear if k > 1 else zfar)

    def arrived(d, k):
        s = slot(d, k)
        remote(blk.at[s], blk.at[s], o_send, g_recv.at[s], partner).wait_recv()

    seen = {True: set(), False: set()}

    def need(d, k):
        if (d, k) == (0, 0):
            return
        todo = [where for where in seen if (d, k) not in seen[where]]
        for where in todo:
            seen[where].add((d, k))
        if len(todo) == 2:
            arrived(d, k)
        elif todo:

            @pl.when(inner if todo[0] else jnp.logical_not(inner))
            def _():
                arrived(d, k)

    def z_out(d):
        z_copy(d, 0).start()

        @pl.when(inner)
        def _():
            z_copy(d, 1).start()

    def own():
        half_copy().start()
        y_copy(0, 0).start()
        z_out(0)
        for j in range(NT):
            amp_copy(j).start()

    def own_second():
        need(1, 0)
        z_out(1)
        y_copy(1, 0).start()

    def z_pass(d, k):
        @pl.when(inner)
        def _():
            arrived(d, k)
            zf_copy(d, k).start()

        seen[True].add((d, k))

    def y_out(d, k):
        need(d, k)
        y_copy(d, k).start()

    def put_amp(q, rows, at, t):
        hi = t.astype(BF)
        tth[q, rows, pl.ds(at, 128)] = hi
        ttl[q, rows, pl.ds(at, 128)] = (t - hi.astype(F32)).astype(BF)

    def prep():
        load_t.wait()

        def body(i, carry):
            at = pl.multiple_of(i * 128, 128)
            put_amp(0, pl.ds(0, IC), at, t32[pl.ds(at, 128), :].T)
            return carry

        lax.fori_loop(0, HR // 128, body, 0)

    def amp(j):
        amp_copy(j).wait_recv()

        def body(i, carry):
            at = pl.multiple_of(i * 128, 128)
            put_amp(1, tile(j), at, tp32[j, pl.ds(at, 128), :].T)
            return carry

        lax.fori_loop(0, HR // 128, body, 0)

    def split(s):
        def body(i, carry):
            at = pl.multiple_of(i * 128, 128)
            m = blk[s, pl.ds(at, 128), :] * mask[half * (HR // 128) + i, s].astype(F32)
            hi = m.astype(BF)
            rhs[s, pl.ds(at, 128), 0:128] = hi
            rhs[s, pl.ds(at, 128), 128:256] = (m - hi.astype(F32)).astype(BF)
            return carry

        lax.fori_loop(0, HR // 128, body, 0)

    def multiply(q, s, j):
        at = pl.ds(pl.multiple_of(j * TI, TI), TI)
        a = jnp.dot(tth[q, at, :], rhs[s], preferred_element_type=F32)
        b = jnp.dot(ttl[q, at, :], rhs[s, :, 0:128], preferred_element_type=F32)
        pbuf[q, s, at, :] = a[:, 0:128] + (a[:, 128:256] + b)

    def keeps(k):
        return (zs[k] + core) % 2 == 0

    def c_copy(q, d, k, j):
        n = d * 2 + k // 2
        return remote(
            pbuf.at[q, slot(d, k), tile(j)],
            crecv.at[q, n, tile(j)],
            c_send.at[q, n, j],
            c_recv.at[q, n, j],
            mate,
        )

    def x_copy(q, d, p, s, j):
        yv = y_of(d)
        place = (x + 4 - yv) % 4 - 1
        to = (yv * 4 + zh * 2 + core, loop)
        return remote(
            pbuf.at[q, s, tile(j)],
            xrecv.at[q, place, p, tile(j)],
            x_send.at[q, d, p, j],
            x_recv.at[q, place, p, j],
            to,
        )

    def to_mate(q, d, k, j):
        @pl.when(jnp.logical_not(keeps(k)))
        def _():
            c_copy(q, d, k, j).start()

    def reduce(q, d, k, j):
        @pl.when(keeps(k))
        def _():
            n = d * 2 + k // 2
            s = slot(d, k)
            c_copy(q, d, k, j).wait_recv()
            pbuf[q, s, tile(j)] = pbuf[q, s, tile(j)] + crecv[q, n, tile(j)]

            @pl.when(x != y_of(d))
            def _():
                x_copy(q, d, k // 2, s, j).start()

    def ready(d, k):
        if (d, k) == (0, 0):
            load_b.wait()
        need(d, k)
        s = slot(d, k)
        split(s)
        return s

    def block(d, k):
        s = ready(d, k)

        def body(j, carry):
            multiply(0, s, j)
            return carry

        lax.fori_loop(0, NT, body, 0)
        for j in range(NT):
            to_mate(0, d, k, j)

    def part(k, j, low, high):
        def body(d, carry):
            multiply(1, slot(d, k), j)
            to_mate(1, d, k, j)
            return carry

        lax.fori_loop(low, high, body, 0)

    def sums(q, ds, ks, js):
        for d in ds:
            for k in ks:
                for j in js:
                    reduce(q, d, k, j)

    def last():
        s = ready(3, 3)
        todo = [(1, 0), (1, 1), (1, 2), (0, 0), (0, 1), (0, 2)]
        for n, (q, j) in enumerate(todo):
            multiply(q, s, j)
            to_mate(q, 3, 3, j)
            if n:
                reduce(todo[n - 1][0], 3, 3, todo[n - 1][1])
        reduce(0, 3, 3, NT - 1)

    def h_copy(s, j):
        return remote(
            pbuf.at[0, s, tile(j)], zrecv.at[tile(j)], h_send.at[j], h_recv.at[j], hpeer
        )

    def s_copy(p, s, j):
        return remote(
            pbuf.at[1, s, tile(j)],
            srecv.at[p, tile(j)],
            s_send.at[p, j],
            s_recv.at[p, j],
            partner,
        )

    def total(q, p):
        s = x * 4 + 2 * ((zq + p) % 2) + core
        for j in range(NT):
            for i in range(3):
                dst = xrecv.at[q, i, p, tile(j)]
                remote(dst, dst, o_send, x_recv.at[q, i, p, j], partner).wait_recv()
            add = (xrecv[q, 0, p, tile(j)] + xrecv[q, 1, p, tile(j)]) + xrecv[
                q, 2, p, tile(j)
            ]
            if q == 1:
                pbuf[1, s, tile(j)] = pbuf[1, s, tile(j)] + add
                s_copy(p, s, j).start()
            else:
                s_copy(p, s, j).wait_recv()
                pbuf[0, s, tile(j)] = (pbuf[0, s, tile(j)] + add) + srecv[p, tile(j)]

                @pl.when((zq + zh + p) % 2 == 1)
                def _():
                    h_copy(s, j).start()

    steps = {
        "own": own,
        "own_second": own_second,
        "z_pass": z_pass,
        "y_out": y_out,
        "prep": prep,
        "amp": amp,
        "block": block,
        "part": part,
        "last": last,
        "sum": sums,
        "total": total,
    }
    for name, *where in ORDER:
        steps[name](*where)
    s_mine = x * 4 + 2 * zh + core
    for j in range(NT):
        h_copy(s_mine, j).wait_recv()
        out[:, j * TI : (j + 1) * TI] = (pbuf[0, s_mine, tile(j)] + zrecv[tile(j)]).T

    sent = [half_copy(), z_copy(0, 0), z_copy(1, 0)]
    for j in range(NT):
        sent += [h_copy(s_mine, j), amp_copy(j)]
        sent += [s_copy(p, s_mine, j) for p in range(2)]
        sent += [c_copy(q, d, 2 * p, j) for q in (0, 1) for d in range(4) for p in (0, 1)]
    sent += [y_copy(d, k) for d in (0, 1) for k in range(4)]
    for c in sent:
        c.wait_send()

    @pl.when(inner)
    def _():
        for d in (0, 1):
            z_copy(d, 1).wait_send()
            for k in (1, 2, 3):
                zf_copy(d, k).wait_send()

    for d in range(4):

        @pl.when(x != y_of(d))
        def _():
            for q in (0, 1):
                for p in (0, 1):
                    for j in range(NT):
                        x_copy(q, d, p, loop, j).wait_send()


def ladder_of(amplitudes, integrals, screen_mask):
    dma = pltpu.SemaphoreType.DMA
    return pl.pallas_call(
        kernel,
        out_shape=jax.ShapeDtypeStruct((TILE, IC), F32),
        in_specs=[
            pl.BlockSpec(memory_space=pl.ANY),
            pl.BlockSpec(memory_space=pl.ANY),
            pl.BlockSpec(memory_space=pltpu.SMEM),
        ],
        out_specs=pl.BlockSpec(memory_space=pltpu.VMEM),
        scratch_shapes=[
            pltpu.VMEM((NL, HR, TILE), F32),
            pltpu.VMEM((HR, IC), F32),
            pltpu.VMEM((NT, HR, TI), F32),
            pltpu.VMEM((2, IC, HR), BF),
            pltpu.VMEM((2, IC, HR), BF),
            pltpu.VMEM((NL, HR, 2 * TILE), BF),
            pltpu.VMEM((2, NL, IC, TILE), F32),
            pltpu.VMEM((2, 8, IC, TILE), F32),
            pltpu.VMEM((2, 3, 2, IC, TILE), F32),
            pltpu.VMEM((2, IC, TILE), F32),
            pltpu.VMEM((IC, TILE), F32),
            dma((2,)),
            dma((NL,)),
            dma,
            dma((NT,)),
            dma((NT,)),
            dma((2, 4)),
            dma((2, 2)),
            dma((2, 3)),
            dma((2, 8, NT)),
            dma((2, 8, NT)),
            dma((2, 4, 2, NT)),
            dma((2, 3, 2, NT)),
            dma((2, NT)),
            dma((2, NT)),
            dma((NT,)),
            dma((NT,)),
        ],
        compiler_params=pltpu.CompilerParams(
            collective_id=0, has_side_effects=True, vmem_limit_bytes=60 * 1024 * 1024
        ),
        cost_estimate=pl.CostEstimate(
            flops=2 * 3 * CR * CR * IC, bytes_accessed=24 * 2**20, transcendentals=0
        ),
    )(amplitudes, integrals, screen_mask)


def on_device(amplitudes, integrals, screen_mask, base_residual, vir_energy, occ_energy):
    ladder = ladder_of(amplitudes, integrals, screen_mask)
    residual = base_residual + ladder
    update = residual / (vir_energy[:, None] + occ_energy[None, :])
    return (residual, update)


def solution(mesh):
    in_specs = (
        P("row", "loop"),
        P("row", "loop"),
        P("row", None),
        P("row", "loop"),
        P("row"),
        P("loop"),
    )
    out_specs = (P("row", "loop"), P("row", "loop"))
    return jax.shard_map(
        on_device, mesh=mesh, in_specs=in_specs, out_specs=out_specs, check_vma=False
    )
```

```python
import jax
import jax.numpy as jnp
from jax import lax
from jax.experimental import pallas as pl
from jax.experimental.pallas import tpu as pltpu
from jax.sharding import PartitionSpec as P

TILE = 128
NL = 16
CR = 2048
HR = CR // 2
IC = 768
TI = 256
NT = IC // TI
BF = jnp.bfloat16
F32 = jnp.float32
MESH = pl.DeviceIdType.MESH

ORDER = [
    ("own",),
    ("prep",),
    ("block", 0, 0),
    ("own_second",),
    ("z_pass", 0, 1),
    ("z_pass", 0, 2),
    ("y_out", 0, 1),
    ("block", 1, 0),
    ("sum", 0, (0,), (0,), (0, 1, 2)),
    ("block", 2, 0),
    ("sum", 0, (1,), (0,), (0, 1, 2)),
    ("block", 0, 1),
    ("sum", 0, (2,), (0,), (0, 1, 2)),
    ("z_pass", 1, 1),
    ("z_pass", 1, 2),
    ("y_out", 1, 1),
    ("block", 3, 0),
    ("sum", 0, (0,), (1,), (0, 1, 2)),
    ("block", 1, 1),
    ("sum", 0, (3,), (0,), (0, 1, 2)),
    ("sum", 0, (1,), (1,), (0, 1, 2)),
    ("amp", 0),
    ("part", 0, 0, 0, 4),
    ("part", 1, 0, 0, 2),
    ("z_pass", 0, 3),
    ("y_out", 0, 2),
    ("sum", 1, (2, 3, 0, 1), (0,), (0,)),
    ("sum", 1, (0, 1), (1,), (0,)),
    ("block", 0, 2),
    ("block", 2, 1),
    ("sum", 0, (0,), (2,), (0, 1, 2)),
    ("sum", 0, (2,), (1,), (0, 1, 2)),
    ("z_pass", 1, 3),
    ("y_out", 1, 2),
    ("block", 3, 1),
    ("z_more",),
    ("block", 1, 2),
    ("sum", 0, (3,), (1,), (0, 1, 2)),
    ("sum", 0, (1,), (2,), (0, 1, 2)),
    ("part", 1, 0, 2, 4),
    ("part", 2, 0, 0, 2),
    ("sum", 1, (2, 3), (1,), (0,)),
    ("sum", 1, (0, 1), (2,), (0,)),
    ("amp", 1),
    ("y_out", 0, 3),
    ("part", 0, 1, 0, 4),
    ("part", 1, 1, 0, 4),
    ("sum", 1, (2, 3, 0, 1), (0, 1), (1,)),
    ("z_pass", 3, 3),
    ("block", 2, 2),
    ("block", 0, 3),
    ("sum", 0, (2,), (2,), (0, 1, 2)),
    ("sum", 0, (0,), (3,), (0, 1, 2)),
    ("part", 2, 1, 0, 3),
    ("part", 2, 0, 2, 3),
    ("part", 3, 0, 0, 1),
    ("part", 3, 1, 0, 1),
    ("sum", 1, (2,), (2,), (0, 1)),
    ("sum", 1, (0, 1), (2,), (1,)),
    ("sum", 1, (0,), (3,), (0, 1)),
    ("block", 3, 2),
    ("block", 1, 3),
    ("sum", 0, (3,), (2,), (0, 1, 2)),
    ("sum", 0, (1,), (3,), (0, 1, 2)),
    ("part", 2, 0, 3, 4),
    ("part", 2, 1, 3, 4),
    ("sum", 1, (3,), (2,), (0, 1)),
    ("part", 3, 0, 1, 2),
    ("part", 3, 1, 1, 2),
    ("sum", 1, (1,), (3,), (0, 1)),
    ("total", 1, 0, (0, 1)),
    ("amp", 2),
    ("part", 0, 2, 0, 4),
    ("part", 1, 2, 0, 4),
    ("sum", 1, (2, 3, 0, 1), (0, 1), (2,)),
    ("total", 0, 0, (0, 1)),
    ("block", 2, 3),
    ("part", 2, 2, 0, 4),
    ("sum", 0, (2,), (3,), (0, 1, 2)),
    ("sum", 1, (2, 3, 0, 1), (2,), (2,)),
    ("part", 3, 2, 0, 3),
    ("part", 3, 0, 2, 3),
    ("part", 3, 1, 2, 3),
    ("sum", 1, (2,), (3,), (0, 1, 2)),
    ("sum", 1, (0, 1), (3,), (2,)),
    ("last",),
    ("total", 1, 0, (2,)),
    ("total", 0, 0, (2,)),
    ("total", 1, 1, (0, 1, 2)),
    ("total", 0, 1, (0, 1, 2)),
]


def kernel(
    amp_hbm,
    int_hbm,
    mask,
    out,
    blk,
    t32,
    tp32,
    tth,
    ttl,
    rhs,
    pbuf,
    crecv,
    xrecv,
    srecv,
    zrecv,
    load_sem,
    g_recv,
    o_send,
    a_send,
    a_recv,
    y_send,
    z_send,
    zf_send,
    c_send,
    c_recv,
    x_send,
    x_recv,
    s_send,
    s_recv,
    h_send,
    h_recv,
):
    row = lax.axis_index("row")
    loop = lax.axis_index("loop")
    x, zh, core = row // 4, (row // 2) % 2, row % 2
    y, z = loop // 4, loop % 4
    half = y // 2
    zq = z // 2
    inner = ((z + 1) // 2) % 2 == 1
    zs = [z, z + 1 - 2 * (z % 2), 2 - zq, 3 - 3 * zq]

    def y_of(d):
        base = y + (d % 2) * (3 - 2 * y)
        return base + (d // 2) * (1 - 2 * (base % 2))

    def slot(d, k):
        return y_of(d) * 4 + zs[k]

    partner = (row, (3 - y) * 4 + z)
    ymate = (row, y_of(2) * 4 + z)
    znear = (row, y * 4 + zs[1])
    zfar = (row, y * 4 + 3 - z)
    mate = (row + 1 - 2 * core, loop)
    hpeer = (row + 2 - 4 * zh, loop)
    mine = pl.ds(pl.multiple_of(half * HR, HR), HR)
    theirs = pl.ds(pl.multiple_of((1 - half) * HR, HR), HR)

    barrier = pltpu.get_barrier_semaphore()
    peers = [partner, ymate, znear, mate, hpeer]
    peers += [(((x + j) % 4) * 4 + zh * 2 + core, loop) for j in (1, 2, 3)]
    for peer in peers:
        pl.semaphore_signal(barrier, inc=1, device_id=peer, device_id_type=MESH)

    @pl.when(inner)
    def _():
        pl.semaphore_signal(barrier, inc=1, device_id=zfar, device_id_type=MESH)

    load_b = pltpu.make_async_copy(int_hbm.at[mine], blk.at[loop], load_sem.at[1])
    load_b.start()
    load_t = pltpu.make_async_copy(amp_hbm.at[mine], t32, load_sem.at[0])
    load_t.start()
    pl.semaphore_wait(barrier, len(peers) + ((z + 1) // 2) % 2)

    def remote(src, dst, send, recv, to):
        return pltpu.make_async_remote_copy(
            src_ref=src,
            dst_ref=dst,
            send_sem=send,
            recv_sem=recv,
            device_id=to,
            device_id_type=MESH,
        )

    def tile(j):
        return pl.ds(j * TI, TI)

    def g_copy(d, k, send, to):
        s = slot(d, k)
        src = int_hbm.at[mine] if (d, k) == (0, 0) else blk.at[s]
        return remote(src, blk.at[s], send, g_recv.at[s], to)

    def half_copy():
        return remote(int_hbm.at[theirs], blk.at[loop], o_send, g_recv.at[loop], partner)

    def amp_copy(j):
        return remote(
            amp_hbm.at[theirs, tile(j)], tp32.at[j], a_send.at[j], a_recv.at[j], partner
        )

    def y_copy(d, k):
        return g_copy(d, k, y_send.at[d, k], ymate)

    def z_copy(d, far):
        return g_copy(d, 0, z_send.at[d, far], zfar if far else znear)

    def zf_copy(d, k):
        return g_copy(d, k, zf_send.at[d, k - 1], znear if k > 1 else zfar)

    def arrived(d, k):
        s = slot(d, k)
        remote(blk.at[s], blk.at[s], o_send, g_recv.at[s], partner).wait_recv()

    seen = {True: set(), False: set()}

    def need(d, k):
        if (d, k) == (0, 0):
            return
        todo = [where for where in seen if (d, k) not in seen[where]]
        for where in todo:
            seen[where].add((d, k))
        if len(todo) == 2:
            arrived(d, k)
        elif todo:

            @pl.when(inner if todo[0] else jnp.logical_not(inner))
            def _():
                arrived(d, k)

    def z_out(d):
        z_copy(d, 0).start()

        @pl.when(inner)
        def _():
            z_copy(d, 1).start()

    def own():
        half_copy().start()
        y_copy(0, 0).start()
        z_out(0)
        for j in range(NT):
            amp_copy(j).start()

    def own_second():
        need(1, 0)
        z_out(1)
        y_copy(1, 0).start()

    def z_pass(d, k):
        @pl.when(inner)
        def _():
            arrived(d, k)
            zf_copy(d, k).start()

        seen[True].add((d, k))

    def z_more():
        @pl.when(inner)
        def _():
            zf_copy(3, 1).start()

    def y_out(d, k):
        need(d, k)
        y_copy(d, k).start()

    def put_amp(q, rows, at, t):
        hi = t.astype(BF)
        tth[q, rows, pl.ds(at, 128)] = hi
        ttl[q, rows, pl.ds(at, 128)] = (t - hi.astype(F32)).astype(BF)

    def prep():
        load_t.wait()

        def body(i, carry):
            at = pl.multiple_of(i * 128, 128)
            put_amp(0, pl.ds(0, IC), at, t32[pl.ds(at, 128), :].T)
            return carry

        lax.fori_loop(0, HR // 128, body, 0)

    def amp(j):
        amp_copy(j).wait_recv()

        def body(i, carry):
            at = pl.multiple_of(i * 128, 128)
            put_amp(1, tile(j), at, tp32[j, pl.ds(at, 128), :].T)
            return carry

        lax.fori_loop(0, HR // 128, body, 0)

    def split(s):
        def body(i, carry):
            at = pl.multiple_of(i * 128, 128)
            m = blk[s, pl.ds(at, 128), :] * mask[half * (HR // 128) + i, s].astype(F32)
            hi = m.astype(BF)
            rhs[s, pl.ds(at, 128), 0:128] = hi
            rhs[s, pl.ds(at, 128), 128:256] = (m - hi.astype(F32)).astype(BF)
            return carry

        lax.fori_loop(0, HR // 128, body, 0)

    def multiply(q, s, j):
        at = pl.ds(pl.multiple_of(j * TI, TI), TI)
        a = jnp.dot(tth[q, at, :], rhs[s], preferred_element_type=F32)
        b = jnp.dot(ttl[q, at, :], rhs[s, :, 0:128], preferred_element_type=F32)
        pbuf[q, s, at, :] = a[:, 0:128] + (a[:, 128:256] + b)

    def keeps(k):
        return (zs[k] + core) % 2 == 0

    def c_copy(q, d, k, j):
        n = d * 2 + k // 2
        return remote(
            pbuf.at[q, slot(d, k), tile(j)],
            crecv.at[q, n, tile(j)],
            c_send.at[q, n, j],
            c_recv.at[q, n, j],
            mate,
        )

    def x_copy(q, d, p, s, j):
        yv = y_of(d)
        place = (x + 4 - yv) % 4 - 1
        to = (yv * 4 + zh * 2 + core, loop)
        return remote(
            pbuf.at[q, s, tile(j)],
            xrecv.at[q, place, p, tile(j)],
            x_send.at[q, d, p, j],
            x_recv.at[q, place, p, j],
            to,
        )

    def to_mate(q, d, k, j):
        @pl.when(jnp.logical_not(keeps(k)))
        def _():
            c_copy(q, d, k, j).start()

    def reduce(q, d, k, j):
        @pl.when(keeps(k))
        def _():
            n = d * 2 + k // 2
            s = slot(d, k)
            c_copy(q, d, k, j).wait_recv()
            pbuf[q, s, tile(j)] = pbuf[q, s, tile(j)] + crecv[q, n, tile(j)]

            @pl.when(x != y_of(d))
            def _():
                x_copy(q, d, k // 2, s, j).start()

    def ready(d, k):
        if (d, k) == (0, 0):
            load_b.wait()
        need(d, k)
        s = slot(d, k)
        split(s)
        return s

    def block(d, k):
        s = ready(d, k)

        def body(j, carry):
            multiply(0, s, j)
            return carry

        lax.fori_loop(0, NT, body, 0)
        for j in range(NT):
            to_mate(0, d, k, j)

    def part(k, j, low, high):
        def body(d, carry):
            multiply(1, slot(d, k), j)
            to_mate(1, d, k, j)
            return carry

        lax.fori_loop(low, high, body, 0)

    def sums(q, ds, ks, js):
        for d in ds:
            for k in ks:
                for j in js:
                    reduce(q, d, k, j)

    def last():
        s = ready(3, 3)
        todo = [(1, 0), (1, 1), (1, 2), (0, 0), (0, 1), (0, 2)]
        for n, (q, j) in enumerate(todo):
            multiply(q, s, j)
            to_mate(q, 3, 3, j)
            if n:
                reduce(todo[n - 1][0], 3, 3, todo[n - 1][1])
        reduce(0, 3, 3, NT - 1)

    def h_copy(s, j):
        return remote(
            pbuf.at[0, s, tile(j)], zrecv.at[tile(j)], h_send.at[j], h_recv.at[j], hpeer
        )

    def s_copy(p, s, j):
        return remote(
            pbuf.at[1, s, tile(j)],
            srecv.at[p, tile(j)],
            s_send.at[p, j],
            s_recv.at[p, j],
            partner,
        )

    def total(q, p, js):
        s = x * 4 + 2 * ((zq + p) % 2) + core
        for j in js:
            for i in range(3):
                dst = xrecv.at[q, i, p, tile(j)]
                remote(dst, dst, o_send, x_recv.at[q, i, p, j], partner).wait_recv()
            add = (xrecv[q, 0, p, tile(j)] + xrecv[q, 1, p, tile(j)]) + xrecv[
                q, 2, p, tile(j)
            ]
            if q == 1:
                pbuf[1, s, tile(j)] = pbuf[1, s, tile(j)] + add
                s_copy(p, s, j).start()
            else:
                s_copy(p, s, j).wait_recv()
                pbuf[0, s, tile(j)] = (pbuf[0, s, tile(j)] + add) + srecv[p, tile(j)]

                @pl.when((zq + zh + p) % 2 == 1)
                def _():
                    h_copy(s, j).start()

    steps = {
        "own": own,
        "own_second": own_second,
        "z_pass": z_pass,
        "z_more": z_more,
        "y_out": y_out,
        "prep": prep,
        "amp": amp,
        "block": block,
        "part": part,
        "last": last,
        "sum": sums,
        "total": total,
    }
    for name, *where in ORDER:
        steps[name](*where)
    s_mine = x * 4 + 2 * zh + core
    for j in range(NT):
        h_copy(s_mine, j).wait_recv()
        out[:, j * TI : (j + 1) * TI] = (pbuf[0, s_mine, tile(j)] + zrecv[tile(j)]).T

    sent = [half_copy(), z_copy(0, 0), z_copy(1, 0)]
    for j in range(NT):
        sent += [h_copy(s_mine, j), amp_copy(j)]
        sent += [s_copy(p, s_mine, j) for p in range(2)]
        sent += [c_copy(q, d, 2 * p, j) for q in (0, 1) for d in range(4) for p in (0, 1)]
    sent += [y_copy(d, k) for d in (0, 1) for k in range(4) if (d, k) != (1, 3)]
    for c in sent:
        c.wait_send()

    @pl.when(inner)
    def _():
        for d in (0, 1):
            z_copy(d, 1).wait_send()
            for k in (1, 2, 3):
                zf_copy(d, k).wait_send()
        zf_copy(3, 1).wait_send()
        zf_copy(3, 3).wait_send()

    for d in range(4):

        @pl.when(x != y_of(d))
        def _():
            for q in (0, 1):
                for p in (0, 1):
                    for j in range(NT):
                        x_copy(q, d, p, loop, j).wait_send()


def ladder_of(amplitudes, integrals, screen_mask):
    dma = pltpu.SemaphoreType.DMA
    return pl.pallas_call(
        kernel,
        out_shape=jax.ShapeDtypeStruct((TILE, IC), F32),
        in_specs=[
            pl.BlockSpec(memory_space=pl.ANY),
            pl.BlockSpec(memory_space=pl.ANY),
            pl.BlockSpec(memory_space=pltpu.SMEM),
        ],
        out_specs=pl.BlockSpec(memory_space=pltpu.VMEM),
        scratch_shapes=[
            pltpu.VMEM((NL, HR, TILE), F32),
            pltpu.VMEM((HR, IC), F32),
            pltpu.VMEM((NT, HR, TI), F32),
            pltpu.VMEM((2, IC, HR), BF),
            pltpu.VMEM((2, IC, HR), BF),
            pltpu.VMEM((NL, HR, 2 * TILE), BF),
            pltpu.VMEM((2, NL, IC, TILE), F32),
            pltpu.VMEM((2, 8, IC, TILE), F32),
            pltpu.VMEM((2, 3, 2, IC, TILE), F32),
            pltpu.VMEM((2, IC, TILE), F32),
            pltpu.VMEM((IC, TILE), F32),
            dma((2,)),
            dma((NL,)),
            dma,
            dma((NT,)),
            dma((NT,)),
            dma((2, 4)),
            dma((2, 2)),
            dma((4, 3)),
            dma((2, 8, NT)),
            dma((2, 8, NT)),
            dma((2, 4, 2, NT)),
            dma((2, 3, 2, NT)),
            dma((2, NT)),
            dma((2, NT)),
            dma((NT,)),
            dma((NT,)),
        ],
        compiler_params=pltpu.CompilerParams(
            collective_id=0, has_side_effects=True, vmem_limit_bytes=60 * 1024 * 1024
        ),
        cost_estimate=pl.CostEstimate(
            flops=2 * 3 * CR * CR * IC, bytes_accessed=24 * 2**20, transcendentals=0
        ),
    )(amplitudes, integrals, screen_mask)


def on_device(amplitudes, integrals, screen_mask, base_residual, vir_energy, occ_energy):
    ladder = ladder_of(amplitudes, integrals, screen_mask)
    residual = base_residual + ladder
    update = residual / (vir_energy[:, None] + occ_energy[None, :])
    return (residual, update)


def solution(mesh):
    in_specs = (
        P("row", "loop"),
        P("row", "loop"),
        P("row", None),
        P("row", "loop"),
        P("row"),
        P("loop"),
    )
    out_specs = (P("row", "loop"), P("row", "loop"))
    return jax.shard_map(
        on_device, mesh=mesh, in_specs=in_specs, out_specs=out_specs, check_vma=False
    )
```

```python
import jax
import jax.numpy as jnp
from jax import lax
from jax.experimental import pallas as pl
from jax.experimental.pallas import tpu as pltpu
from jax.sharding import PartitionSpec as P

TILE = 128
NL = 16
CR = 2048
HR = CR // 2
IC = 768
TI = 256
NT = IC // TI
BF = jnp.bfloat16
F32 = jnp.float32
MESH = pl.DeviceIdType.MESH

ORDER = [
    ("own",),
    ("prep",),
    ("block", 0, 0),
    ("own_second",),
    ("z_pass", 0, 1),
    ("z_pass", 0, 2),
    ("y_out", 0, 1),
    ("block", 1, 0),
    ("sum", 0, (0,), (0,), (0, 1, 2)),
    ("block", 2, 0),
    ("sum", 0, (1,), (0,), (0, 1, 2)),
    ("block", 0, 1),
    ("sum", 0, (2,), (0,), (0, 1, 2)),
    ("z_pass", 1, 1),
    ("z_pass", 1, 2),
    ("y_out", 1, 1),
    ("block", 3, 0),
    ("sum", 0, (0,), (1,), (0, 1, 2)),
    ("block", 1, 1),
    ("sum", 0, (3,), (0,), (0, 1, 2)),
    ("sum", 0, (1,), (1,), (0, 1, 2)),
    ("amp", 0),
    ("part", 0, 0, 0, 4),
    ("part", 1, 0, 0, 2),
    ("z_pass", 0, 3),
    ("y_out", 0, 2),
    ("sum", 1, (2, 0, 3, 1), (0,), (0,)),
    ("sum", 1, (0, 1), (1,), (0,)),
    ("block", 0, 2),
    ("block", 2, 1),
    ("sum", 0, (0,), (2,), (0, 1, 2)),
    ("sum", 0, (2,), (1,), (0, 1, 2)),
    ("z_pass", 1, 3),
    ("y_out", 1, 2),
    ("block", 3, 1),
    ("z_more",),
    ("block", 1, 2),
    ("sum", 0, (3,), (1,), (0, 1, 2)),
    ("sum", 0, (1,), (2,), (0, 1, 2)),
    ("part", 1, 0, 2, 4),
    ("part", 2, 0, 0, 2),
    ("sum", 1, (2, 3), (1,), (0,)),
    ("sum", 1, (0, 1), (2,), (0,)),
    ("amp", 1),
    ("y_out", 0, 3),
    ("part", 0, 1, 0, 4),
    ("part", 1, 1, 0, 4),
    ("sum", 1, (2, 0, 3, 1), (0, 1), (1,)),
    ("z_pass", 3, 3),
    ("block", 2, 2),
    ("block", 0, 3),
    ("sum", 0, (2,), (2,), (0, 1, 2)),
    ("sum", 0, (0,), (3,), (0, 1, 2)),
    ("part", 2, 1, 0, 3),
    ("part", 2, 0, 2, 3),
    ("part", 3, 0, 0, 1),
    ("part", 3, 1, 0, 1),
    ("sum", 1, (2,), (2,), (0, 1)),
    ("sum", 1, (0, 1), (2,), (1,)),
    ("sum", 1, (0,), (3,), (0, 1)),
    ("block", 3, 2),
    ("block", 1, 3),
    ("sum", 0, (3,), (2,), (0, 1, 2)),
    ("sum", 0, (1,), (3,), (0, 1, 2)),
    ("part", 2, 0, 3, 4),
    ("part", 2, 1, 3, 4),
    ("sum", 1, (3,), (2,), (0, 1)),
    ("part", 3, 0, 1, 2),
    ("part", 3, 1, 1, 2),
    ("sum", 1, (1,), (3,), (0, 1)),
    ("total", 1, 0, (0, 1)),
    ("amp", 2),
    ("part", 0, 2, 0, 4),
    ("part", 1, 2, 0, 4),
    ("sum", 1, (2, 0, 3, 1), (0, 1), (2,)),
    ("total", 0, 0, (0, 1)),
    ("block", 2, 3),
    ("part", 2, 2, 0, 4),
    ("sum", 0, (2,), (3,), (0, 1, 2)),
    ("sum", 1, (2, 0, 3, 1), (2,), (2,)),
    ("part", 3, 2, 0, 3),
    ("part", 3, 0, 2, 3),
    ("part", 3, 1, 2, 3),
    ("sum", 1, (2,), (3,), (0, 1, 2)),
    ("sum", 1, (0, 1), (3,), (2,)),
    ("last",),
    ("total", 1, 0, (2,)),
    ("total", 1, 1, (0, 1, 2)),
    ("total", 0, 0, (2,)),
    ("total", 0, 1, (0, 1, 2)),
]


def kernel(
    amp_hbm,
    int_hbm,
    mask,
    out,
    blk,
    t32,
    tp32,
    tth,
    ttl,
    rhs,
    pbuf,
    crecv,
    xrecv,
    srecv,
    zrecv,
    load_sem,
    g_recv,
    o_send,
    a_send,
    a_recv,
    y_send,
    z_send,
    zf_send,
    c_send,
    c_recv,
    x_send,
    x_recv,
    s_send,
    s_recv,
    h_send,
    h_recv,
):
    row = lax.axis_index("row")
    loop = lax.axis_index("loop")
    x, zh, core = row // 4, (row // 2) % 2, row % 2
    y, z = loop // 4, loop % 4
    half = y // 2
    zq = z // 2
    inner = ((z + 1) // 2) % 2 == 1
    zs = [z, z + 1 - 2 * (z % 2), 2 - zq, 3 - 3 * zq]

    def y_of(d):
        base = y + (d % 2) * (3 - 2 * y)
        return base + (d // 2) * (1 - 2 * (base % 2))

    def slot(d, k):
        return y_of(d) * 4 + zs[k]

    partner = (row, (3 - y) * 4 + z)
    ymate = (row, y_of(2) * 4 + z)
    znear = (row, y * 4 + zs[1])
    zfar = (row, y * 4 + 3 - z)
    mate = (row + 1 - 2 * core, loop)
    hpeer = (row + 2 - 4 * zh, loop)
    mine = pl.ds(pl.multiple_of(half * HR, HR), HR)
    theirs = pl.ds(pl.multiple_of((1 - half) * HR, HR), HR)

    barrier = pltpu.get_barrier_semaphore()
    peers = [partner, ymate, znear, mate, hpeer]
    peers += [(((x + j) % 4) * 4 + zh * 2 + core, loop) for j in (1, 2, 3)]
    for peer in peers:
        pl.semaphore_signal(barrier, inc=1, device_id=peer, device_id_type=MESH)

    @pl.when(inner)
    def _():
        pl.semaphore_signal(barrier, inc=1, device_id=zfar, device_id_type=MESH)

    load_b = pltpu.make_async_copy(int_hbm.at[mine], blk.at[loop], load_sem.at[1])
    load_b.start()
    load_t = pltpu.make_async_copy(amp_hbm.at[mine], t32, load_sem.at[0])
    load_t.start()
    pl.semaphore_wait(barrier, len(peers) + ((z + 1) // 2) % 2)

    def remote(src, dst, send, recv, to):
        return pltpu.make_async_remote_copy(
            src_ref=src,
            dst_ref=dst,
            send_sem=send,
            recv_sem=recv,
            device_id=to,
            device_id_type=MESH,
        )

    def tile(j):
        return pl.ds(j * TI, TI)

    def g_copy(d, k, send, to):
        s = slot(d, k)
        src = int_hbm.at[mine] if (d, k) == (0, 0) else blk.at[s]
        return remote(src, blk.at[s], send, g_recv.at[s], to)

    def half_copy():
        return remote(int_hbm.at[theirs], blk.at[loop], o_send, g_recv.at[loop], partner)

    def amp_copy(j):
        return remote(
            amp_hbm.at[theirs, tile(j)], tp32.at[j], a_send.at[j], a_recv.at[j], partner
        )

    def y_copy(d, k):
        return g_copy(d, k, y_send.at[d, k], ymate)

    def z_copy(d, far):
        return g_copy(d, 0, z_send.at[d, far], zfar if far else znear)

    def zf_copy(d, k):
        return g_copy(d, k, zf_send.at[d, k - 1], znear if k > 1 else zfar)

    def arrived(d, k):
        s = slot(d, k)
        remote(blk.at[s], blk.at[s], o_send, g_recv.at[s], partner).wait_recv()

    seen = {True: set(), False: set()}

    def need(d, k):
        if (d, k) == (0, 0):
            return
        todo = [where for where in seen if (d, k) not in seen[where]]
        for where in todo:
            seen[where].add((d, k))
        if len(todo) == 2:
            arrived(d, k)
        elif todo:

            @pl.when(inner if todo[0] else jnp.logical_not(inner))
            def _():
                arrived(d, k)

    def z_out(d):
        z_copy(d, 0).start()

        @pl.when(inner)
        def _():
            z_copy(d, 1).start()

    def own():
        half_copy().start()
        y_copy(0, 0).start()
        z_out(0)
        for j in range(NT):
            amp_copy(j).start()

    def own_second():
        need(1, 0)
        z_out(1)
        y_copy(1, 0).start()

    def z_pass(d, k):
        @pl.when(inner)
        def _():
            arrived(d, k)
            zf_copy(d, k).start()

        seen[True].add((d, k))

    def z_more():
        @pl.when(inner)
        def _():
            zf_copy(3, 1).start()

    def y_out(d, k):
        need(d, k)
        y_copy(d, k).start()

    def put_amp(q, rows, at, t):
        hi = t.astype(BF)
        tth[q, rows, pl.ds(at, 128)] = hi
        ttl[q, rows, pl.ds(at, 128)] = (t - hi.astype(F32)).astype(BF)

    def prep():
        load_t.wait()

        def body(i, carry):
            at = pl.multiple_of(i * 128, 128)
            put_amp(0, pl.ds(0, IC), at, t32[pl.ds(at, 128), :].T)
            return carry

        lax.fori_loop(0, HR // 128, body, 0)

    def amp(j):
        amp_copy(j).wait_recv()

        def body(i, carry):
            at = pl.multiple_of(i * 128, 128)
            put_amp(1, tile(j), at, tp32[j, pl.ds(at, 128), :].T)
            return carry

        lax.fori_loop(0, HR // 128, body, 0)

    def split(s):
        def body(i, carry):
            at = pl.multiple_of(i * 128, 128)
            m = blk[s, pl.ds(at, 128), :] * mask[half * (HR // 128) + i, s].astype(F32)
            hi = m.astype(BF)
            rhs[s, pl.ds(at, 128), 0:128] = hi
            rhs[s, pl.ds(at, 128), 128:256] = (m - hi.astype(F32)).astype(BF)
            return carry

        lax.fori_loop(0, HR // 128, body, 0)

    def multiply(q, s, j):
        at = pl.ds(pl.multiple_of(j * TI, TI), TI)
        a = jnp.dot(tth[q, at, :], rhs[s], preferred_element_type=F32)
        b = jnp.dot(ttl[q, at, :], rhs[s, :, 0:128], preferred_element_type=F32)
        pbuf[q, s, at, :] = a[:, 0:128] + (a[:, 128:256] + b)

    def keeps(k):
        return (zs[k] + core) % 2 == 0

    def c_copy(q, d, k, j):
        n = d * 2 + k // 2
        return remote(
            pbuf.at[q, slot(d, k), tile(j)],
            crecv.at[q, n, tile(j)],
            c_send.at[q, n, j],
            c_recv.at[q, n, j],
            mate,
        )

    def x_copy(q, d, p, s, j):
        yv = y_of(d)
        place = (x + 4 - yv) % 4 - 1
        to = (yv * 4 + zh * 2 + core, loop)
        return remote(
            pbuf.at[q, s, tile(j)],
            xrecv.at[q, place, p, tile(j)],
            x_send.at[q, d, p, j],
            x_recv.at[q, place, p, j],
            to,
        )

    def to_mate(q, d, k, j):
        @pl.when(jnp.logical_not(keeps(k)))
        def _():
            c_copy(q, d, k, j).start()

    def reduce(q, d, k, j):
        @pl.when(keeps(k))
        def _():
            n = d * 2 + k // 2
            s = slot(d, k)
            c_copy(q, d, k, j).wait_recv()
            pbuf[q, s, tile(j)] = pbuf[q, s, tile(j)] + crecv[q, n, tile(j)]

            @pl.when(x != y_of(d))
            def _():
                x_copy(q, d, k // 2, s, j).start()

    def ready(d, k):
        if (d, k) == (0, 0):
            load_b.wait()
        need(d, k)
        s = slot(d, k)
        split(s)
        return s

    def block(d, k):
        s = ready(d, k)

        def body(j, carry):
            multiply(0, s, j)
            return carry

        lax.fori_loop(0, NT, body, 0)
        for j in range(NT):
            to_mate(0, d, k, j)

    def part(k, j, low, high):
        def body(d, carry):
            multiply(1, slot(d, k), j)
            to_mate(1, d, k, j)
            return carry

        lax.fori_loop(low, high, body, 0)

    def sums(q, ds, ks, js):
        for k in ks:
            for j in js:
                for d in ds:
                    reduce(q, d, k, j)

    def last():
        s = ready(3, 3)
        todo = [(1, 0), (1, 1), (1, 2), (0, 0), (0, 1), (0, 2)]
        for n, (q, j) in enumerate(todo):
            multiply(q, s, j)
            to_mate(q, 3, 3, j)
            if n >= 3:
                reduce(todo[n - 3][0], 3, 3, todo[n - 3][1])
        for q, j in todo[3:]:
            reduce(q, 3, 3, j)

    def h_copy(s, j):
        return remote(
            pbuf.at[0, s, tile(j)], zrecv.at[tile(j)], h_send.at[j], h_recv.at[j], hpeer
        )

    def s_copy(p, s, j):
        return remote(
            pbuf.at[1, s, tile(j)],
            srecv.at[p, tile(j)],
            s_send.at[p, j],
            s_recv.at[p, j],
            partner,
        )

    def total(q, p, js):
        s = x * 4 + 2 * ((zq + p) % 2) + core
        for j in js:
            for i in range(3):
                dst = xrecv.at[q, i, p, tile(j)]
                remote(dst, dst, o_send, x_recv.at[q, i, p, j], partner).wait_recv()
            add = (xrecv[q, 0, p, tile(j)] + xrecv[q, 1, p, tile(j)]) + xrecv[
                q, 2, p, tile(j)
            ]
            if q == 1:
                pbuf[1, s, tile(j)] = pbuf[1, s, tile(j)] + add
                s_copy(p, s, j).start()
            else:
                s_copy(p, s, j).wait_recv()
                pbuf[0, s, tile(j)] = (pbuf[0, s, tile(j)] + add) + srecv[p, tile(j)]

                @pl.when((zq + zh + p) % 2 == 1)
                def _():
                    h_copy(s, j).start()

    steps = {
        "own": own,
        "own_second": own_second,
        "z_pass": z_pass,
        "z_more": z_more,
        "y_out": y_out,
        "prep": prep,
        "amp": amp,
        "block": block,
        "part": part,
        "last": last,
        "sum": sums,
        "total": total,
    }
    for name, *where in ORDER:
        steps[name](*where)
    s_mine = x * 4 + 2 * zh + core
    for j in range(NT):
        h_copy(s_mine, j).wait_recv()
        out[:, j * TI : (j + 1) * TI] = (pbuf[0, s_mine, tile(j)] + zrecv[tile(j)]).T

    sent = [half_copy(), z_copy(0, 0), z_copy(1, 0)]
    for j in range(NT):
        sent += [h_copy(s_mine, j), amp_copy(j)]
        sent += [s_copy(p, s_mine, j) for p in range(2)]
        sent += [c_copy(q, d, 2 * p, j) for q in (0, 1) for d in range(4) for p in (0, 1)]
    sent += [y_copy(d, k) for d in (0, 1) for k in range(4) if (d, k) != (1, 3)]
    for c in sent:
        c.wait_send()

    @pl.when(inner)
    def _():
        for d in (0, 1):
            z_copy(d, 1).wait_send()
            for k in (1, 2, 3):
                zf_copy(d, k).wait_send()
        zf_copy(3, 1).wait_send()
        zf_copy(3, 3).wait_send()

    for d in range(4):

        @pl.when(x != y_of(d))
        def _():
            for q in (0, 1):
                for p in (0, 1):
                    for j in range(NT):
                        x_copy(q, d, p, loop, j).wait_send()


def ladder_of(amplitudes, integrals, screen_mask):
    dma = pltpu.SemaphoreType.DMA
    return pl.pallas_call(
        kernel,
        out_shape=jax.ShapeDtypeStruct((TILE, IC), F32),
        in_specs=[
            pl.BlockSpec(memory_space=pl.ANY),
            pl.BlockSpec(memory_space=pl.ANY),
            pl.BlockSpec(memory_space=pltpu.SMEM),
        ],
        out_specs=pl.BlockSpec(memory_space=pltpu.VMEM),
        scratch_shapes=[
            pltpu.VMEM((NL, HR, TILE), F32),
            pltpu.VMEM((HR, IC), F32),
            pltpu.VMEM((NT, HR, TI), F32),
            pltpu.VMEM((2, IC, HR), BF),
            pltpu.VMEM((2, IC, HR), BF),
            pltpu.VMEM((NL, HR, 2 * TILE), BF),
            pltpu.VMEM((2, NL, IC, TILE), F32),
            pltpu.VMEM((2, 8, IC, TILE), F32),
            pltpu.VMEM((2, 3, 2, IC, TILE), F32),
            pltpu.VMEM((2, IC, TILE), F32),
            pltpu.VMEM((IC, TILE), F32),
            dma((2,)),
            dma((NL,)),
            dma,
            dma((NT,)),
            dma((NT,)),
            dma((2, 4)),
            dma((2, 2)),
            dma((4, 3)),
            dma((2, 8, NT)),
            dma((2, 8, NT)),
            dma((2, 4, 2, NT)),
            dma((2, 3, 2, NT)),
            dma((2, NT)),
            dma((2, NT)),
            dma((NT,)),
            dma((NT,)),
        ],
        compiler_params=pltpu.CompilerParams(
            collective_id=0, has_side_effects=True, vmem_limit_bytes=60 * 1024 * 1024
        ),
        cost_estimate=pl.CostEstimate(
            flops=2 * 3 * CR * CR * IC, bytes_accessed=24 * 2**20, transcendentals=0
        ),
    )(amplitudes, integrals, screen_mask)


def on_device(amplitudes, integrals, screen_mask, base_residual, vir_energy, occ_energy):
    ladder = ladder_of(amplitudes, integrals, screen_mask)
    residual = base_residual + ladder
    update = residual / (vir_energy[:, None] + occ_energy[None, :])
    return (residual, update)


def solution(mesh):
    in_specs = (
        P("row", "loop"),
        P("row", "loop"),
        P("row", None),
        P("row", "loop"),
        P("row"),
        P("loop"),
    )
    out_specs = (P("row", "loop"), P("row", "loop"))
    return jax.shard_map(
        on_device, mesh=mesh, in_specs=in_specs, out_specs=out_specs, check_vma=False
    )
```
